32 devices in a mesh: grp: 2 (over y), rows: 4 (over z), img: 2 (over x), tp: 2 (over core).
Axes of the slice: x: 2, y: 2, z: 4, core: 2. Of those that a mesh axis runs over, the one named last changes fastest.
Arguments:
- features: bfloat16 [16, 28, 2, 7168], P(('grp', 'img'), 'rows', 'tp'), parts along dimension 0, may hold values from -8 to 8
- gn_gain: float32 [128], P('tp'), may hold values from 0.5 to 1.5
- conv_w: bfloat16 [3, 3, 3, 128], P(None, None, None, 'tp'), may hold values from -0.1875 to 0.1875
- patch_w: bfloat16 [1280, 588], P('rows'), may hold values from -0.25 to 0.25
- pos_emb: bfloat16 [64, 1280], replicated, may hold values from -3 to 3
- ln1_gain: float32 [1280], replicated, may hold values from 0.5 to 1.5
- qkv_w: bfloat16 [1280, 3, 1280], P('rows', None, 'tp'), may hold values from -3 to 3
- out_w: bfloat16 [1280, 1280], P('rows', 'tp'), may hold values from -0.15625 to 0.15625
- final_gain: float32 [1280], replicated, may hold values from 0.5 to 1.5
- head_w: float32 [1280], replicated, may hold values from -0.15625 to 0.15625
- owner_slot: int32 [4, 4], P(('grp', 'img')), parts along dimension 0, may hold values from 0 to 3, each once within a row
Outputs:
- grad_features: bfloat16 [16, 28, 2, 7168], P(('grp', 'img'), 'rows', 'tp'), parts along dimension 0
- slot_reward: float32 [16], P(('grp', 'img', 'rows')), parts along dimension 0
The draws below stay inside these ranges and needn't reach their ends.
There are 2 independent parts, one for each index of `grp`. The reference program is written for one: setup_inputs(seed, part) draws one part's arguments, and reference() takes and returns one part's arrays. A program takes and returns all parts, laid end to end along the dimension named above; an argument that names none is the same for every part. Nothing has to cross between parts.
Inputs may be any that keep to these rules, and one draw needn't show every extreme that they name: Each row is a permutation: image g * 4 + j is scored in slot owner_slot[g, j] of its image group.
All inputs are finite; a program needn't handle non-finite values.
Results may differ from the reference program's by a relative error of at most 0.028.
Values may be sent and summed in bfloat16 or wider, within the bound.
A program may use at most 128 MiB of HBM per device.

```python
import math
import jax
import jax.numpy as jnp
from jax import lax

C = 128
GROUPS = 32
D = 1280
HEADS = 16
PATCH = 14
HALF_C = 64
HEAD_DIM = 80
H = 28
W = 112
TOKENS = 64
PIX = 588
IMG_SLAB = 4
IMAGES = 8
N_IMG = 2


def draw_features(key, part):
    noise_key = jax.random.fold_in(key, 0)
    full_shape = (IMAGES, H, W, C)
    position = jnp.arange(H, dtype=jnp.float32) / (H - 1)
    noise_draw = jax.random.normal(noise_key, full_shape, jnp.float32)
    row_scale = 0.5 + position
    values = noise_draw * row_scale[None, :, None, None]
    values = jnp.clip(values, -8.0, 8.0)
    values = values.reshape(IMAGES, H, W, 2, HALF_C).transpose(0, 1, 3, 2, 4).reshape(IMAGES, H, 2, W * HALF_C)
    return values.astype(jnp.bfloat16)


def draw_qkv_w(key, part):
    base_key = jax.random.fold_in(key, 0)
    weights = jax.random.normal(base_key, (D, 3, HEADS, HEAD_DIM), jnp.float32)
    weights = jnp.clip(weights, -3.0, 3.0) / jnp.sqrt(jnp.float32(D))
    return weights.reshape(D, 3, HEADS * HEAD_DIM).astype(jnp.bfloat16)


def steps_of(key, extent, shards, least, top_value):
    factor_of, own = 1.0, jax.random.fold_in(key, 6)
    for axis_at, blocks in shards:
        steps = jnp.exp(jax.random.uniform(jax.random.fold_in(own, axis_at), (blocks,), jnp.float32, least / len(shards), top_value / len(shards)))
        factor_of = factor_of * jnp.repeat(steps, extent[axis_at] // blocks).reshape([-1 if axis == axis_at else 1 for axis in range(len(extent))])
    return factor_of


def bell_draw(stream_key, dims, scale, bound, pieces=(), held_as=jnp.bfloat16):
    values = scale * jax.random.normal(stream_key, dims, jnp.float32)
    if pieces:
        values = values * steps_of(stream_key, dims, pieces, -0.22, 0.18)
    return jnp.clip(values, -bound, bound).astype(held_as)


def setup_inputs(seed: int = 0, part: int = 0) -> dict:
    key_list = jax.random.split(jax.random.key(seed), 12)
    part_keys = jax.random.split(jax.random.fold_in(key_list[11], part), 12)
    features = draw_features(jax.random.fold_in(jax.random.fold_in(key_list[11], part), 71), part)
    gn_gain = jnp.clip(1.0 + 0.1 * jax.random.normal(key_list[1], (C,), jnp.float32), 0.5, 1.5)
    conv_w = bell_draw(key_list[2], (3, 3, 3, C), (9 * C) ** -0.5, 0.1875, ((3, 2),))
    patch_w = bell_draw(key_list[3], (D, PIX), PIX ** -0.5, 0.25, ((0, 4),))
    pos_emb = bell_draw(key_list[4], (TOKENS, D), 0.5, 3.0)
    ln1_gain = jnp.clip(1.0 + 0.1 * jax.random.normal(key_list[5], (D,), jnp.float32), 0.5, 1.5)
    qkv_w = draw_qkv_w(jax.random.fold_in(key_list[11], 71), part)
    out_w = bell_draw(key_list[7], (D, HEADS * HEAD_DIM), D ** -0.5, 0.15625, ((0, 4), (1, 2)))
    final_gain = jnp.clip(1.0 + 0.1 * jax.random.normal(key_list[8], (D,), jnp.float32), 0.5, 1.5)
    head_w = bell_draw(key_list[9], (D,), D ** -0.5, 0.15625, (), jnp.float32)
    owner_slot = jax.vmap(lambda own: jax.random.permutation(own, IMG_SLAB))(jax.random.split(part_keys[10], N_IMG)).reshape((N_IMG, IMG_SLAB)).astype(jnp.int32)
    return dict(features=features, gn_gain=gn_gain, conv_w=conv_w, patch_w=patch_w, pos_emb=pos_emb, ln1_gain=ln1_gain, qkv_w=qkv_w, out_w=out_w, final_gain=final_gain, head_w=head_w, owner_slot=owner_slot)


EPS_GROUP = 1e-06
EPS_LAYER = 1e-05

def round_half(values):
    return lax.optimization_barrier(values.astype(jnp.bfloat16)).astype(jnp.float32)

def layer_norm(values, scale_vec):
    average = lax.optimization_barrier(jnp.mean(values, axis=-1, keepdims=True))
    centred = values - average
    spread = lax.optimization_barrier(jnp.mean(centred * centred, axis=-1, keepdims=True))
    inverse = lax.rsqrt(spread + EPS_LAYER)
    normed = centred * inverse
    return (normed * scale_vec, normed, inverse)

def layer_norm_back(upstream, normed, inverse, scale_vec):
    scaled = upstream * scale_vec
    mean_one = lax.optimization_barrier(jnp.mean(scaled, axis=-1, keepdims=True))
    mean_two = lax.optimization_barrier(jnp.mean(scaled * normed, axis=-1, keepdims=True))
    return inverse * (scaled - mean_one - normed * mean_two)

def silu_parts(values):
    sigmoid = jax.nn.sigmoid(values)
    return (values * sigmoid, sigmoid * (1.0 + values * (1.0 - sigmoid)))

def group_sums(values, groups_here):
    grouped = values.reshape(values.shape[0], -1, groups_here, values.shape[3] // groups_here)
    return lax.optimization_barrier(jnp.sum(grouped, axis=(1, 3)))

def spread_groups(per_group, chan_count):
    return jnp.repeat(per_group, chan_count // per_group.shape[1], axis=1)[:, None, None, :]

def conv_forward(rim_rows, kernel):
    image_count, rows_rim, col_count, chan_count = rim_rows.shape
    rows_here = rows_rim - 2
    padded = jnp.pad(rim_rows, ((0, 0), (0, 0), (1, 1), (0, 0)))
    accum = jnp.zeros((image_count * rows_here * col_count, 3), jnp.float32)
    for offset_y in range(3):
        for offset_x in range(3):
            window = padded[:, offset_y:offset_y + rows_here, offset_x:offset_x + col_count, :]
            accum = accum + jnp.dot(window.reshape(-1, chan_count), kernel[:, offset_y, offset_x, :].T, preferred_element_type=jnp.float32)
    return accum.reshape(image_count, rows_here, col_count, 3)

def conv_back(grad_rim, kernel):
    image_count, rows_rim, col_count, _ = grad_rim.shape
    rows_here = rows_rim - 2
    padded = jnp.pad(grad_rim, ((0, 0), (0, 0), (1, 1), (0, 0)))
    accum = jnp.zeros((image_count * rows_here * col_count, kernel.shape[3]), jnp.float32)
    for offset_y in range(3):
        for offset_x in range(3):
            window = padded[:, 2 - offset_y:2 - offset_y + rows_here, 2 - offset_x:2 - offset_x + col_count, :]
            accum = accum + jnp.dot(window.reshape(-1, 3), kernel[:, offset_y, offset_x, :], preferred_element_type=jnp.float32)
    return accum.reshape(image_count, rows_here, col_count, kernel.shape[3])

def to_patches(picture):
    larger = jnp.repeat(jnp.repeat(picture, 2, axis=0), 2, axis=1)
    patch_rows = larger.shape[0] // PATCH
    patch_cols = larger.shape[1] // PATCH
    blocks = larger.reshape(patch_rows, PATCH, patch_cols, PATCH, 3).transpose(0, 2, 1, 3, 4)
    return blocks.reshape(patch_rows * patch_cols, PATCH * PATCH * 3)

def from_patches(grads_in, rows_full, col_count):
    patch_rows = rows_full * 2 // PATCH
    patch_cols = col_count * 2 // PATCH
    blocks = grads_in.reshape(patch_rows, patch_cols, PATCH, PATCH, 3).transpose(0, 2, 1, 3, 4)
    larger = blocks.reshape(rows_full, 2, col_count, 2, 3)
    return lax.optimization_barrier(jnp.sum(larger, axis=(1, 3)))

def soft_weights(q_heads, k_heads):
    factor = 1.0 / math.sqrt(HEAD_DIM)
    scores = jnp.einsum('thd,shd->hts', q_heads, k_heads) * factor
    row_max = lax.optimization_barrier(jnp.max(scores, axis=-1, keepdims=True))
    exp_scores = jnp.exp(scores - row_max)
    return exp_scores / lax.optimization_barrier(jnp.sum(exp_scores, axis=-1, keepdims=True))

def split_heads(rows_in):
    return rows_in.reshape(rows_in.shape[0], rows_in.shape[1] // HEAD_DIM, HEAD_DIM).astype(jnp.float32)

def attend(queries, key_rows, value_rows):
    prob_soft = soft_weights(split_heads(queries), split_heads(key_rows))
    attended = jnp.einsum('hts,shd->thd', round_half(prob_soft), split_heads(value_rows))
    return attended.reshape(queries.shape).astype(jnp.bfloat16)

def attend_back(queries, key_rows, value_rows, head_grad):
    factor = 1.0 / math.sqrt(HEAD_DIM)
    q_heads = split_heads(queries)
    k_heads = split_heads(key_rows)
    v_heads = split_heads(value_rows)
    g_heads = split_heads(head_grad)
    prob_soft = soft_weights(q_heads, k_heads)
    dprob = jnp.einsum('thd,shd->hts', g_heads, v_heads)
    dvalue = jnp.einsum('hts,thd->shd', round_half(prob_soft), g_heads).reshape(queries.shape).astype(jnp.bfloat16)
    dscores = prob_soft * (dprob - lax.optimization_barrier(jnp.sum(dprob * prob_soft, axis=-1, keepdims=True))) * factor
    dscores = round_half(dscores)
    dquery = jnp.einsum('hts,shd->thd', dscores, k_heads).reshape(queries.shape).astype(jnp.bfloat16)
    dkey = jnp.einsum('hts,thd->shd', dscores, q_heads).reshape(queries.shape).astype(jnp.bfloat16)
    return (dquery, dkey, dvalue)

def reference(features, gn_gain, conv_w, patch_w, pos_emb, ln1_gain, qkv_w, out_w, final_gain, head_w, owner_slot):
    half_heads = D // 2
    half_chan = C // 2
    qkv_flat = qkv_w.reshape(D, 3, D)
    out_flat = out_w.reshape(D, D)
    count_group = H * W * (C // GROUPS)
    feat_maps = features.reshape(IMAGES, H, 2, W, HALF_C).transpose(0, 1, 3, 2, 4).reshape(IMAGES, H, W, C)

    def one_image(feat_one):
        feat_float = feat_one.astype(jnp.float32)[None]
        totals = group_sums(feat_float, GROUPS)
        squares_sum = group_sums(feat_float * feat_float, GROUPS)
        average = totals / count_group
        inverse = lax.rsqrt(squares_sum / count_group - average * average + EPS_GROUP)
        normed = (feat_float - spread_groups(average, C)) * spread_groups(inverse, C)
        scaled = normed * gn_gain
        active, slope_silu = silu_parts(scaled)
        active = active.astype(jnp.bfloat16)
        rim_rows = jnp.pad(active, ((0, 0), (1, 1), (0, 0), (0, 0)))
        picture = jnp.zeros((1, H, W, 3), jnp.float32)
        for half_idx in range(2):
            chan_slice = slice(half_idx * half_chan, (half_idx + 1) * half_chan)
            picture = picture + round_half(conv_forward(rim_rows[..., chan_slice], conv_w[..., chan_slice]))
        picture = picture.astype(jnp.bfloat16)[0]
        patches = to_patches(picture)
        embedded = jnp.dot(patches, patch_w.T, preferred_element_type=jnp.float32) + pos_emb.astype(jnp.float32)
        normed_in, hat_in, inv_in = layer_norm(embedded, ln1_gain)
        normed_round = normed_in.astype(jnp.bfloat16)
        mixed_out = jnp.zeros((TOKENS, D), jnp.float32)
        stored = []
        for half_idx in range(2):
            col_slice = slice(half_idx * half_heads, (half_idx + 1) * half_heads)
            queries = jnp.dot(normed_round, qkv_flat[:, 0, col_slice], preferred_element_type=jnp.float32).astype(jnp.bfloat16)
            key_rows = jnp.dot(normed_round, qkv_flat[:, 1, col_slice], preferred_element_type=jnp.float32).astype(jnp.bfloat16)
            value_rows = jnp.dot(normed_round, qkv_flat[:, 2, col_slice], preferred_element_type=jnp.float32).astype(jnp.bfloat16)
            attended = attend(queries, key_rows, value_rows)
            mixed_out = mixed_out + round_half(jnp.dot(attended, out_flat[:, col_slice].T, preferred_element_type=jnp.float32))
            stored.append((queries, key_rows, value_rows))
        residual_out = embedded + mixed_out
        pooled = lax.optimization_barrier(jnp.mean(residual_out, axis=0))
        pooled_out, hat_z, inv_z = layer_norm(pooled, final_gain)
        reward = jnp.sum(pooled_out * head_w)
        upstream = layer_norm_back(head_w, hat_z, inv_z, final_gain)
        row_round = upstream.astype(jnp.bfloat16)[None, :]
        dnormed = jnp.zeros((TOKENS, D), jnp.float32)
        for half_idx in range(2):
            col_slice = slice(half_idx * half_heads, (half_idx + 1) * half_heads)
            queries, key_rows, value_rows = stored[half_idx]
            head_grad = jnp.dot(row_round, out_flat[:, col_slice], preferred_element_type=jnp.float32).astype(jnp.bfloat16)
            head_grad = jnp.broadcast_to(head_grad, queries.shape)
            dquery, dkey, dvalue = attend_back(queries, key_rows, value_rows, head_grad)
            partial_value = jnp.dot(dquery, qkv_flat[:, 0, col_slice].T, preferred_element_type=jnp.float32)
            partial_value = partial_value + jnp.dot(dkey, qkv_flat[:, 1, col_slice].T, preferred_element_type=jnp.float32)
            partial_value = partial_value + jnp.dot(dvalue, qkv_flat[:, 2, col_slice].T, preferred_element_type=jnp.float32)
            dnormed = dnormed + round_half(partial_value)
        dembedded = upstream[None, :] + layer_norm_back(dnormed, hat_in, inv_in, ln1_gain)
        dpatches = jnp.dot(dembedded.astype(jnp.bfloat16), patch_w, preferred_element_type=jnp.float32)
        dpicture = from_patches(dpatches, H, W).astype(jnp.bfloat16)
        grad_rim = jnp.pad(dpicture[None], ((0, 0), (1, 1), (0, 0), (0, 0)))
        dactive = conv_back(grad_rim, conv_w)
        gated_grad = dactive * slope_silu * gn_gain
        back_one = group_sums(gated_grad, GROUPS) / count_group
        back_two = group_sums(gated_grad * normed, GROUPS) / count_group
        grad_one = spread_groups(inverse, C) * (gated_grad - spread_groups(back_one, C) - normed * spread_groups(back_two, C))
        return (reward, grad_one[0].astype(jnp.bfloat16))
    rewards, grad_maps = lax.map(one_image, feat_maps)
    grad_features = grad_maps.reshape(IMAGES, H, W, 2, HALF_C).transpose(0, 1, 3, 2, 4).reshape(IMAGES, H, 2, W * HALF_C)
    group_base = jnp.arange(IMAGES, dtype=jnp.int32) // IMG_SLAB * IMG_SLAB
    slot_index = (owner_slot.reshape(IMAGES).astype(jnp.int32) + group_base).astype(jnp.int32)
    slot_reward = jnp.zeros_like(rewards).at[slot_index].set(rewards)
    return (grad_features, slot_reward)
```

```python
import functools
import math

import jax
import jax.numpy as jnp
import numpy as np
from jax import lax
from jax.experimental import pallas as pl
from jax.experimental.pallas import tpu as pltpu
from jax.sharding import PartitionSpec as P

C = 128
GROUPS = 32
PATCH = 14
HEAD_DIM = 80
W = 112
CHUNK = 14
CHUNKS = W // CHUNK
ROWS = 7
CELL = 160
EPS_GROUP = 1e-06
EPS_LAYER = 1e-05
F32 = jnp.float32
BF16 = jnp.bfloat16
EXACT = lax.Precision.HIGHEST


def up(count, step):
    return (count + step - 1) // step * step


def mm(left, right, left_dim=1, right_dim=0, precision=None):
    return lax.dot_general(
        left, right, (((left_dim,), (right_dim,)), ((), ())),
        preferred_element_type=F32, precision=precision,
    )


def split(values):
    high = values.astype(BF16)
    return high, (values - high.astype(F32)).astype(BF16)


class Sizes:
    def __init__(self, slab, rows_devices, planes, tp, width, span, heads, half_width):
        self.slab = slab
        self.rows_devices = rows_devices
        self.planes = planes
        self.tp = tp
        self.layer = planes * tp
        self.width = width
        self.span = span
        self.heads = heads
        self.half_width = half_width
        self.tokens = rows_devices * 2 * CHUNKS
        self.own = width // rows_devices
        self.ones = CELL + self.tokens
        self.k = up(up(self.ones + rows_devices, 16 * rows_devices), 256)
        self.part = self.k // rows_devices
        self.pack = up(3 * span, 128)
        self.win = up(min(self.own + 127, width), 128)
        self.slab8 = 8 * slab
        self.prow = up(planes, 8)


def tables(z):
    fold = np.zeros((3 * PATCH * PATCH, z.k), np.float32)
    for entry in range(3 * PATCH * PATCH):
        pixel, colour = divmod(entry, 3)
        row, col = divmod(pixel, PATCH)
        fold[entry, colour * 49 + row // 2 * 7 + col // 2] = 1
    place_f = np.zeros((32, 18 * 128), np.float32)
    place_b = np.zeros((256, 7 * 64), np.float32)
    for colour in range(3):
        for ky in range(3):
            for kx in range(3):
                tap = colour * 9 + ky * 3 + kx
                for xx in range(CHUNK):
                    lane = 42 * ky + 14 * colour + xx
                    place_f[tap, (xx + kx + 1) * 128 + lane] = 1
                    out = xx + kx - 1
                    if 0 <= out < CHUNK:
                        place_b[lane, out // 2 * 64 + out % 2 * 32 + tap] = 1
                if kx == 2:
                    place_b[128 + 42 * ky + 14 * colour + 13, tap] = 1
                if kx == 0:
                    place_b[128 + 42 * ky + 14 * colour, 6 * 64 + 32 + tap] = 1
    cell = np.zeros((384, 2 * z.k), np.float32)
    for half in range(2):
        for row in range(ROWS):
            for colour in range(3):
                for col in range(7):
                    line = row + 1
                    cell[line // 3 * 128 + line % 3 * 42 + colour * 14 + half * 7 + col,
                         half * z.k + colour * 49 + row * 7 + col] = 1
    rd = z.rows_devices
    hot = np.zeros((z.tokens, z.k), np.float32)
    for half in range(2):
        for r in range(rd):
            for c in range(CHUNKS):
                hot[half * rd * CHUNKS + r * CHUNKS + c, CELL + r * 2 * CHUNKS + 2 * c + half] = 1
    selpos = np.zeros((z.tokens, z.k), np.float32)
    selpos[np.arange(z.tokens), CELL + np.arange(z.tokens)] = 1
    pick = np.zeros((z.pack, 3 * z.heads * 128), np.float32)
    for which in range(3):
        for head in range(z.heads):
            for lane in range(HEAD_DIM):
                pick[which * z.span + head * HEAD_DIM + lane, (which * z.heads + head) * 128 + lane] = 1
    group = np.zeros((128, 128), np.float32)
    lanes = np.arange(128)
    group[lanes[:, None] % 64 // 4 == lanes[None, :] % 64 // 4] = 1
    rowsel = np.zeros((2 * z.slab, 2 * z.slab8), np.float32)
    for s in range(z.slab):
        for y in range(ROWS):
            rowsel[s, y * z.slab + s] = 1
            rowsel[z.slab + s, z.slab8 + y * z.slab + s] = 1
    bf = lambda a: jnp.asarray(a, BF16)
    return [bf(fold), bf(place_f), bf(place_b), bf(cell), bf(hot), bf(selpos), bf(pick),
            jnp.asarray(group, F32), jnp.asarray(rowsel, F32)]


class Sender:
    def __init__(self, sems):
        self.send, self.recv = sems
        self.copies = []

    def start(self, src, dst, where):
        at = len(self.copies)
        copy = pltpu.make_async_remote_copy(
            src_ref=src, dst_ref=dst, send_sem=self.send.at[at], recv_sem=self.recv.at[at],
            device_id=where, device_id_type=pl.DeviceIdType.MESH,
        )
        copy.start()
        self.copies.append(copy)

    def arrive(self):
        for copy in self.copies:
            copy.wait_recv()

    def finish(self):
        for copy in self.copies:
            copy.wait_send()


def kernel(
    z, split_axes, split_sizes,
    feat_hbm, gn_ref, conv_ref, patch_hbm, pos_ref, ln1_ref, qkv_hbm, out_hbm, fin_ref, head_ref, slot_ref,
    fold_hbm, placef_hbm, placeb_hbm, cell_hbm, hot_ref, selpos_ref, pick_hbm, group_ref, rowsel_ref,
    grad_ref, reward_ref,
    feat, patch, qkvw, outw, fold, placef, placeb, cell, pick,
    xs, slope, act, cwf, bandf, bandb, tmp_t, out1, sb1, p1, pics, pp,
    stat_own, stat_buf, mean_own, mean_buf, ypart, rsbuf, yfull, yh, eprime, owin, posw, dmat,
    aaug, am, qkv, prob, att, mx_own, mx, dqkv, dpart, dbuf, sb2, b1, dact, bs_own, bs_buf,
    invs, share, uk,
    local_sems, *remote,
):
    sems = [Sender(remote[2 * i : 2 * i + 2]) for i in range(len(remote) // 2)]
    s_stat, s_mean, s_rs, s_ag, s_e, s_o, s_1, s_2, s_mix, s_b2, s_b1, s_bst = sems
    rd, slab, tokens, k = z.rows_devices, z.slab, z.tokens, z.k
    planes, heads, span = z.planes, z.heads, z.span
    me = lax.axis_index("rows")
    plane = 0
    for axis, size in zip(split_axes, split_sizes):
        plane = plane * size + lax.axis_index(axis)
    tp = lax.axis_index("tp")
    lay = plane * z.tp + tp

    def column(offset):
        index = lax.rem(me + offset, rd)
        return index, {"rows": index}

    def neighbour(offset):
        index = lax.rem(lay + offset, z.layer)
        where = {"tp": lax.rem(index, z.tp)}
        rest = index // z.tp
        for axis, size in reversed(list(zip(split_axes, split_sizes))):
            where[axis] = lax.rem(rest, size)
            rest = rest // size
        return index, where

    barrier = pltpu.get_barrier_semaphore()
    for offset in range(1, rd):
        pl.semaphore_signal(barrier, inc=1, device_id=column(offset)[1], device_id_type=pl.DeviceIdType.MESH)
    for offset in range(1, z.layer):
        pl.semaphore_signal(barrier, inc=1, device_id=neighbour(offset)[1], device_id_type=pl.DeviceIdType.MESH)

    start = jnp.minimum(plane * span // 128 * 128, z.half_width - 256)
    start = pl.multiple_of(start, 128)
    inside = plane * span - start
    window = pl.ds(start, 256)
    loads = []

    def load(src, dst):
        copy = pltpu.make_async_copy(src, dst, local_sems.at[len(loads)])
        copy.start()
        loads.append(copy)
        return copy

    l_feat = load(feat_hbm, feat)
    l_patch = load(patch_hbm, patch)
    l_fold = load(fold_hbm, fold)
    l_qkv = load(qkv_hbm.at[:, :, window], qkvw)
    l_pf = load(placef_hbm, placef)
    l_out = load(out_hbm.at[:, window], outw)
    l_pb = load(placeb_hbm, placeb)
    l_pick = load(pick_hbm, pick)
    l_cell = load(cell_hbm, cell)

    flat = CHUNKS * CHUNK * 64
    wide = CHUNK * 64
    used = ROWS * slab
    count = rd * ROWS * W * (C // GROUPS)

    def total_rows(first, second):
        return mm(rowsel_ref[...], jnp.concatenate([first, second], axis=0), precision=EXACT)

    def lanes_sum(values):
        total = values[:, 0:128]
        for block in range(1, values.shape[1] // 128):
            total = total + values[:, block * 128 : block * 128 + 128]
        return total

    l_feat.wait()
    xs[used:, :] = jnp.zeros((z.slab8 - used, flat), F32)
    for y in range(ROWS):
        xs[y * slab : y * slab + slab, :] = feat[y].astype(F32)

    def stats(c, carry):
        x = xs[:, pl.ds(pl.multiple_of(c * wide, 128), wide)]
        return carry[0] + lanes_sum(x), carry[1] + lanes_sum(x * x)

    zero = jnp.zeros((z.slab8, 128), F32)
    first, second = lax.fori_loop(0, CHUNKS, stats, (zero, zero))
    stat_own[...] = total_rows(first, second)
    pl.semaphore_wait(barrier, rd - 1 + z.layer - 1)
    for offset in range(1, rd):
        index, where = column(offset)
        s_stat.start(stat_own, stat_buf.at[me], where)
    stat_buf[me] = stat_own[...]

    begin = me * z.own
    wstart = jnp.minimum(begin // 128 * 128, z.width - z.win)
    wstart = pl.multiple_of(wstart, 128)
    wlanes = pl.ds(wstart, z.win)
    posw[:, :k] = mm(pos_ref[:, wlanes], selpos_ref[...], 0, 0)
    gains = jnp.broadcast_to(ln1_ref[:, wlanes], (8, z.win)) * 0.125
    posw[:, k:] = mm(gains, jnp.ones((8, 128), F32), 0, 0, EXACT)
    own_rows = pl.ds(pl.multiple_of(begin - wstart, 16), z.own)
    l_patch.wait()
    l_fold.wait()
    e_own = mm(patch[...], fold[...]) + posw[own_rows, :k]
    mean = jnp.mean(e_own, axis=0, keepdims=True)
    mean_own[...] = jnp.broadcast_to(mean, (8, k))
    lane_k = lax.broadcasted_iota(jnp.int32, (1, k), 1)
    e_own = e_own - mean + (lane_k == z.ones + me).astype(F32)
    gcol = posw[own_rows, k:]
    e_rows = pl.ds(pl.multiple_of(begin, 16), z.own)
    eprime[e_rows, :] = e_own.astype(BF16)
    e_gain = (e_own * jnp.concatenate([gcol] * (k // 128), axis=1)).astype(BF16)
    l_qkv.wait()
    blocks = [jnp.zeros((k, 128), F32) for _ in range(z.pack // 128)]
    lane256 = lax.broadcasted_iota(jnp.int32, (1, 256), 1)
    for which in range(3):
        part = mm(e_gain, qkvw[which], 0, 0)
        base, off = divmod(span * which, 128)
        part = pltpu.roll(part, lax.rem(off - inside + 512, 256), 1)
        part = jnp.where((lane256 >= off) & (lane256 < off + span), part, 0.0)
        blocks[base] = blocks[base] + part[:, :128]
        if off + span > 128:
            blocks[base + 1] = blocks[base + 1] + part[:, 128:]
    ypart[...] = jnp.concatenate(blocks, axis=1).astype(BF16)

    def part_rows(index):
        return pl.ds(pl.multiple_of(index * z.part, 16), z.part)

    for offset in range(1, rd):
        index, where = column(offset)
        s_rs.start(ypart.at[part_rows(index)], rsbuf.at[me], where)
    rsbuf[me] = ypart[part_rows(me), :]
    for offset in range(1, rd):
        index, where = column(offset)
        s_mean.start(mean_own, mean_buf.at[me], where)
    mean_buf[me] = mean_own[...]
    for offset in range(1, rd):
        index, where = column(offset)
        s_e.start(eprime.at[e_rows], eprime.at[e_rows], where)
    l_out.wait()
    ow = outw[...].astype(F32)
    pieces = []
    for head in range(heads):
        moved = pltpu.roll(ow, lax.rem(512 - inside - head * HEAD_DIM, 256), 1)[:, :128]
        pieces.append(jnp.where(lane256[:, :128] < HEAD_DIM, moved, 0.0))
    owin[e_rows, :] = (jnp.concatenate(pieces, axis=1) if heads > 1 else pieces[0]).astype(BF16)
    for offset in range(1, rd):
        index, where = column(offset)
        s_o.start(owin.at[e_rows], owin.at[e_rows], where)

    cwf[...] = jnp.zeros((32, 128), F32)
    for colour in range(3):
        for ky in range(3):
            cwf[pl.ds(9 * colour + 3 * ky, 3), 0:64] = conv_ref[colour, ky].astype(F32)
    taps = cwf[...]
    l_pf.wait()
    spread = mm(taps[:, :64].astype(BF16), placef[...], 0, 0).astype(BF16)
    for px in range(18):
        bandf[px * 64 : px * 64 + 64, :] = spread[:, px * 128 : px * 128 + 128]
    act[:, 0:128] = jnp.zeros((z.slab8, 128), BF16)
    act[:, 128 + flat :] = jnp.zeros((z.slab8, 128), BF16)

    s_stat.arrive()

    def tile(per_image):
        return jnp.concatenate([jnp.concatenate([per_image] * 8, axis=0)] * CHUNK_BLOCKS, axis=1)

    CHUNK_BLOCKS = wide // 128
    gain = jnp.concatenate([gn_ref[...], gn_ref[...]], axis=1)
    gain_wide = jnp.concatenate([gain] * CHUNK_BLOCKS, axis=1)

    def group_means(buf):
        total = buf[0]
        for r in range(1, rd):
            total = total + buf[r]
        return mm(total, group_ref[...], precision=EXACT) * (1.0 / count)

    both = group_means(stat_buf)
    average = both[:slab]
    inverse = lax.rsqrt(both[slab:] - average * average + EPS_GROUP)
    average_t = jnp.concatenate([average] * 8, axis=0)
    inverse_t = jnp.concatenate([inverse] * 8, axis=0)

    def activate(c, carry):
        at = pl.ds(pl.multiple_of(c * wide, 128), wide)
        x = xs[:, at]
        avg = jnp.concatenate([average_t] * CHUNK_BLOCKS, axis=1)
        inv = jnp.concatenate([inverse_t] * CHUNK_BLOCKS, axis=1)
        normed = (x - avg) * inv
        scaled = normed * gain_wide
        sig = 0.5 * jnp.tanh(0.5 * scaled) + 0.5
        xs[:, at] = normed
        active = scaled * sig
        act[:, pl.ds(pl.multiple_of(c * wide + 128, 128), wide)] = active.astype(BF16)
        slope[:, at] = sig * (1.0 + scaled - active) * gain_wide
        return carry

    lax.fori_loop(0, CHUNKS, activate, 0)
    lhs = jnp.concatenate([act[:, wide * c : wide * c + wide + 256] for c in range(CHUNKS)], axis=0)
    tmp_t[...] = mm(lhs, bandf[...])
    lane = lax.broadcasted_iota(jnp.int32, (8, 128), 1)

    def slot_mask(slot):
        return (lane >= 42 * slot) & (lane < 42 * slot + 42)

    masks = [slot_mask(j) for j in range(3)]

    def message(s, carry):
        acc = [jnp.zeros((8, 128), F32) for _ in range(3)]
        for y in range(ROWS):
            value = tmp_t[pl.ds(y * slab + s, 8, stride=z.slab8), :]
            for ky in range(3):
                block, j = divmod(y - ky + 2, 3)
                shift = 42 * (j - ky) % 128
                moved = value if shift == 0 else pltpu.roll(value, shift, 1)
                acc[block] = acc[block] + jnp.where(masks[j], moved, 0.0)
        out1[s] = jnp.concatenate(acc, axis=1)
        return carry

    for s in range(slab):
        message(s, 0)
    for slot in range(slab):
        source = 0
        for j in range(slab):
            source = jnp.where(slot_ref[0, j] == slot, j, source)
        sb1[slot] = out1[source]
    for offset in range(1, rd):
        index, where = column(offset)
        s_1.start(sb1.at[index], p1.at[me], where)
    p1[me] = sb1[me]

    s_rs.arrive()
    total = rsbuf[0].astype(F32)
    for r in range(1, rd):
        total = total + rsbuf[r].astype(F32)
    yfull[part_rows(me), :] = total.astype(BF16)
    for offset in range(1, rd):
        index, where = column(offset)
        s_ag.start(yfull.at[part_rows(me)], yfull.at[part_rows(me)], where)

    l_pb.wait()
    cwf[...] = jnp.zeros((32, 128), F32)
    tap64 = taps[:, :64]
    none = jnp.zeros((32, 64), F32)
    double = jnp.concatenate(
        [jnp.concatenate([tap64, none], axis=1), jnp.concatenate([none, tap64], axis=1)], axis=0
    ).astype(BF16)
    for pair in range(7):
        bandb[:, pair * 128 : pair * 128 + 128] = mm(
            placeb[:, pair * 64 : pair * 64 + 64], double
        ).astype(BF16)

    s_1.arrive()
    slabs = [p1[r] for r in range(rd)]
    keep = [lane >= 42, lane >= 0, lane < 84]
    for r in range(rd):
        parts = [jnp.where(keep[b], slabs[r][:, b * 128 : b * 128 + 128], 0.0) for b in range(3)]
        parts[1] = jnp.where(lane < 126, parts[1], 0.0)
        parts[0] = jnp.where(lane < 126, parts[0], 0.0)
        if r > 0:
            parts[0] = parts[0] + jnp.where(masks[1], pltpu.roll(slabs[r - 1][:, 256:384], 86, 1), 0.0)
        if r < rd - 1:
            parts[2] = parts[2] + jnp.where(masks[1], pltpu.roll(slabs[r + 1][:, 0:128], 42, 1), 0.0)
        tmp_t[pl.ds(r * 8, 8), :] = parts[0]
        tmp_t[pl.ds(rd * 8 + r * 8, 8), :] = parts[1]
        tmp_t[pl.ds(2 * rd * 8 + r * 8, 8), :] = parts[2]
    half_rows = rd * CHUNKS
    pp[...] = jnp.concatenate(
        [tmp_t[b * half_rows : b * half_rows + half_rows, :] for b in range(3)], axis=1
    ).astype(BF16)
    for offset in range(1, z.layer):
        index, where = neighbour(offset)
        s_2.start(pp, pics.at[lay], where)
    pics[lay] = pp[...]

    s_mean.arrive()
    dmat[...] = jnp.zeros((k, k), F32)
    middle = mean_buf[0][0:1]
    for r in range(1, rd):
        middle = middle + mean_buf[r][0:1]
    middle = middle * (1.0 / rd)
    for r in range(rd):
        dmat[z.ones + r : z.ones + r + 1, :] = mean_buf[r][0:1] - middle
    dm = dmat[...].astype(BF16)
    l_pick.wait()
    l_cell.wait()
    s_ag.arrive()
    yh[...] = mm(yfull[...], pick[...]).astype(BF16)
    s_e.arrive()
    gram_high, gram_low = split(mm(eprime[...], eprime[...], 0, 0))

    s_2.arrive()
    rows_all = planes * tokens
    picture = jnp.concatenate(
        [
            sum(pics[pi * z.tp + t].astype(F32) for t in range(z.tp)).astype(BF16)
            for pi in range(planes)
        ],
        axis=0,
    )
    halves = [mm(picture, cell[:, h * k : h * k + k]) for h in range(2)]
    hot = hot_ref[...].astype(F32)
    pieces = []
    for pi in range(planes):
        for h in range(2):
            pieces.append(
                halves[h][pi * half_rows : pi * half_rows + half_rows]
                + hot[h * half_rows : h * half_rows + half_rows]
            )
    cells = jnp.concatenate(pieces, axis=0)
    aug = (cells + mm(cells.astype(BF16), dm, 1, 1)).astype(BF16)
    aaug[...] = aug
    am[...] = mm(aug, gram_high) + mm(aug, gram_low)
    spread_in = jnp.sum(am[...] * aug.astype(F32), axis=1, keepdims=True) * (1.0 / z.width)
    inv_in = lax.rsqrt(jnp.maximum(spread_in, 0.0) + EPS_LAYER)
    invs[...] = jnp.broadcast_to(inv_in, (rows_all, 128))
    qkv[...] = (mm(aug, yh[...]) * inv_in).astype(BF16)

    unit = heads * tokens
    factor = 1.0 / math.sqrt(HEAD_DIM)
    row_u = lax.broadcasted_iota(jnp.int32, (unit, unit), 0)
    col_u = lax.broadcasted_iota(jnp.int32, (unit, unit), 1)
    same = row_u < 0
    for head in range(heads):
        low, high = head * tokens, head * tokens + tokens
        same = same | ((row_u >= low) & (row_u < high) & (col_u >= low) & (col_u < high))
    lane_u = lax.broadcasted_iota(jnp.int32, (1, unit), 1)

    def stacked(ref, pi, which):
        parts = [
            ref[pi * tokens : pi * tokens + tokens, (which * heads + h) * 128 : (which * heads + h) * 128 + 128]
            for h in range(heads)
        ]
        return jnp.concatenate(parts, axis=0) if heads > 1 else parts[0]

    for pi in range(planes):
        scores = mm(stacked(qkv, pi, 0), stacked(qkv, pi, 1), 1, 1) * factor
        if heads > 1:
            scores = jnp.where(same, scores, -1e30)
        top = jnp.max(scores, axis=1, keepdims=True)
        grown = jnp.exp(scores - top)
        soft = grown / jnp.sum(grown, axis=1, keepdims=True)
        prob[pi] = soft
        col_mean = jnp.sum(soft.astype(BF16).astype(F32), axis=0, keepdims=True) * (1.0 / tokens)
        per_head = jnp.concatenate(
            [
                jnp.where((lane_u >= h * tokens) & (lane_u < h * tokens + tokens), col_mean, 0.0)
                for h in range(heads)
            ]
            + [jnp.zeros((8 - heads, unit), F32)],
            axis=0,
        )
        high, low = split(per_head)
        value = stacked(qkv, pi, 2)
        result = mm(high, value) + mm(low, value)
        for h in range(heads):
            att[pi : pi + 1, h * 128 : h * 128 + 128] = result[h : h + 1]
    s_o.arrive()
    if z.prow > planes:
        att[planes:, :] = jnp.zeros((z.prow - planes, heads * 128), F32)
    high, low = split(att[...])
    both = mm(jnp.concatenate([high, low], axis=0), owin[...], 1, 1)
    mx_own[...] = both[: z.prow] + both[z.prow :]
    for offset in range(1, z.layer):
        index, where = neighbour(offset)
        s_mix.start(mx_own, mx.at[lay], where)
    mx[lay] = mx_own[...]
    means = [
        jnp.mean(aaug[pi * tokens : pi * tokens + tokens, :].astype(F32), axis=0, keepdims=True)
        for pi in range(planes)
    ]
    if z.prow > planes:
        means.append(jnp.zeros((z.prow - planes, k), F32))
    high, low = split(jnp.concatenate(means, axis=0))
    both = mm(jnp.concatenate([high, low], axis=0), eprime[...], 1, 1)
    pooled = both[: z.prow] + both[z.prow :]

    s_mix.arrive()
    for index in range(z.layer):
        pooled = pooled + mx[index]
    final_gain, head_w = fin_ref[...], head_ref[...]
    centred = pooled - jnp.mean(pooled, axis=1, keepdims=True)
    inv_z = lax.rsqrt(jnp.mean(centred * centred, axis=1, keepdims=True) + EPS_LAYER)
    hat_z = centred * inv_z
    rewards = jnp.sum(hat_z * final_gain * head_w, axis=1, keepdims=True)
    mine = lax.broadcasted_iota(jnp.int32, (z.prow, 1), 0) == plane
    reward_ref[...] = jnp.sum(jnp.where(mine, rewards, 0.0), axis=0, keepdims=True)
    query = head_w * final_gain
    upstream = inv_z * (
        query - jnp.mean(query, axis=1, keepdims=True) - hat_z * jnp.mean(query * hat_z, axis=1, keepdims=True)
    )
    up16 = upstream.astype(BF16)
    share[...] = mm(up16, owin[...])
    uk[...] = mm(up16, eprime[...]) * (lay == 0).astype(F32)

    for pi in range(planes):
        q, key, value = (stacked(qkv, pi, which) for which in range(3))
        soft = prob[pi]
        parts = [
            jnp.broadcast_to(share[pi : pi + 1, h * 128 : h * 128 + 128], (tokens, 128)) for h in range(heads)
        ]
        given = (jnp.concatenate(parts, axis=0) if heads > 1 else parts[0]).astype(BF16)
        dprob = mm(given, value, 1, 1)
        dscores = (soft * (dprob - jnp.sum(dprob * soft, axis=1, keepdims=True)) * factor).astype(BF16)
        grads = [mm(dscores, key), mm(dscores, q, 0, 0), mm(soft.astype(BF16), given, 0, 0)]
        for which in range(3):
            for h in range(heads):
                dqkv[
                    pi * tokens : pi * tokens + tokens,
                    (which * heads + h) * 128 : (which * heads + h) * 128 + 128,
                ] = grads[which][h * tokens : h * tokens + tokens].astype(BF16)
    back = dqkv[...]
    inv_in = invs[:, 0:1]
    mean_two = jnp.sum(back.astype(F32) * qkv[...].astype(F32), axis=1, keepdims=True) * (1.0 / z.width)
    zk = inv_in * (mm(back, yh[...], 1, 1) - (mean_two * inv_in) * am[...])
    zk = zk + jnp.concatenate(
        [jnp.broadcast_to(uk[pi : pi + 1, :], (tokens, k)) for pi in range(planes)], axis=0
    )
    dcells = (zk + mm(zk.astype(BF16), dm)).astype(BF16)
    dpic = None
    for h in range(2):
        rows = jnp.concatenate(
            [dcells[pi * tokens + h * half_rows : pi * tokens + h * half_rows + half_rows] for pi in range(planes)],
            axis=0,
        )
        term = mm(rows, cell[:, h * k : h * k + k], 1, 1)
        dpic = term if dpic is None else dpic + term
    for pi in range(planes):
        dpart[pi] = dpic[pi * half_rows : pi * half_rows + half_rows].astype(BF16)
    for offset in range(1, z.layer):
        index, where = neighbour(offset)
        s_b2.start(dpart.at[index // z.tp], dbuf.at[lay], where)
    dbuf[lay] = dpart[plane]
    s_b2.arrive()
    total = dbuf[0].astype(F32)
    for index in range(1, z.layer):
        total = total + dbuf[index].astype(F32)
    total = total.astype(BF16).astype(F32)
    for r in range(rd):
        parts = [total[r * 8 : r * 8 + 8, b * 128 : b * 128 + 128] for b in range(3)]
        if r > 0:
            above = total[r * 8 - 8 : r * 8, 256:384]
            parts[0] = parts[0] + jnp.where(masks[0], pltpu.roll(above, 86, 1), 0.0)
        if r < rd - 1:
            below = total[r * 8 + 8 : r * 8 + 16, 0:128]
            parts[2] = parts[2] + jnp.where(masks[2], pltpu.roll(below, 42, 1), 0.0)
        sb2[r] = jnp.concatenate(parts, axis=1)
    for offset in range(1, rd):
        index, where = column(offset)
        s_b1.start(sb2.at[index], b1.at[me], where)
    b1[me] = sb2[me]
    s_b1.arrive()

    image_rows = slab * 8
    grads = jnp.concatenate([b1[slot_ref[0, j]] for j in range(slab)], axis=0)
    lane_s = lax.broadcasted_iota(jnp.int32, (image_rows, 128), 1)
    chunk_s = lax.rem(lax.broadcasted_iota(jnp.int32, (image_rows, 128), 0), 8)
    column_s = lax.rem(lane_s, CHUNK)
    from_left = (column_s == CHUNK - 1) & (chunk_s > 0)
    from_right = (column_s == 0) & (chunk_s < CHUNKS - 1)
    lines = []
    for y in range(ROWS):
        main = jnp.zeros((image_rows, 128), F32)
        for ky in range(3):
            block, j = divmod(y + 2 - ky, 3)
            shift = 42 * (ky - j) % 128
            moved = grads[:, block * 128 : block * 128 + 128]
            moved = moved if shift == 0 else pltpu.roll(moved, shift, 1)
            main = main + jnp.where((lane_s >= 42 * ky) & (lane_s < 42 * ky + 42), moved, 0.0)
        rim = jnp.where(from_left, pltpu.roll(main, 1, 0), 0.0)
        rim = jnp.where(from_right, pltpu.roll(main, image_rows - 1, 0), rim)
        lines.append(jnp.concatenate([main, rim], axis=1).astype(BF16))
    lines.append(jnp.zeros((image_rows, 256), BF16))
    lhs = jnp.concatenate(lines, axis=0)
    spread = mm(lhs, bandb[...])
    for block in range(CHUNK_BLOCKS):
        dact[block] = spread[:, block * 128 : block * 128 + 128]

    def gate(c, carry):
        at = pl.ds(pl.multiple_of(c * wide, 128), wide)
        parts = [
            dact[block, pl.ds(c, z.slab8, stride=8), :] for block in range(CHUNK_BLOCKS)
        ]
        gated = jnp.concatenate(parts, axis=1) * slope[:, at]
        slope[:, at] = gated
        return carry[0] + lanes_sum(gated), carry[1] + lanes_sum(gated * xs[:, at])

    first, second = lax.fori_loop(0, CHUNKS, gate, (zero, zero))
    bs_own[...] = total_rows(first, second)
    for offset in range(1, rd):
        index, where = column(offset)
        s_bst.start(bs_own, bs_buf.at[me], where)
    bs_buf[me] = bs_own[...]
    s_bst.arrive()
    both = group_means(bs_buf)
    one_t = jnp.concatenate([both[:slab]] * 8, axis=0)
    two_t = jnp.concatenate([both[slab:]] * 8, axis=0)

    def finish(c, carry):
        at = pl.ds(pl.multiple_of(c * wide, 128), wide)
        one = jnp.concatenate([one_t] * CHUNK_BLOCKS, axis=1)
        two = jnp.concatenate([two_t] * CHUNK_BLOCKS, axis=1)
        inv = jnp.concatenate([inverse_t] * CHUNK_BLOCKS, axis=1)
        value = inv * (slope[:, at] - one - xs[:, at] * two)
        for y in range(ROWS):
            grad_ref[y, :, at] = value[y * slab : y * slab + slab].astype(BF16)
        return carry

    lax.fori_loop(0, CHUNKS, finish, 0)
    for sender in sems:
        sender.finish()


def body(features, gn_gain, conv_w, patch_w, pos_emb, ln1_gain, qkv_w, out_w, final_gain, head_w, owner_slot):
    slab = features.shape[0]
    rd = lax.axis_size("rows")
    tp = lax.axis_size("tp")
    half_width = qkv_w.shape[2]
    heads_half = half_width // HEAD_DIM
    split_axes = ("grp", "img")
    if heads_half % (lax.axis_size("grp") * lax.axis_size("img")):
        split_axes = ("img",)
    split_sizes = tuple(lax.axis_size(axis) for axis in split_axes)
    planes = math.prod(split_sizes)
    heads = heads_half // planes
    z = Sizes(slab, rd, planes, tp, pos_emb.shape[1], heads * HEAD_DIM, heads, half_width)
    flat = features.shape[3]
    vmem = pl.BlockSpec(memory_space=pltpu.VMEM)
    anys = pl.BlockSpec(memory_space=pl.ANY)
    smem = pl.BlockSpec(memory_space=pltpu.SMEM)
    args = [
        (jnp.transpose(features.reshape(slab, ROWS, flat), (1, 0, 2)), anys),
        (gn_gain.reshape(1, -1), vmem),
        (conv_w, vmem),
        (patch_w, anys),
        (pos_emb, vmem),
        (ln1_gain.reshape(1, -1), vmem),
        (jnp.transpose(qkv_w, (1, 0, 2)), anys),
        (out_w, anys),
        (final_gain.reshape(1, -1), vmem),
        (head_w.reshape(1, -1), vmem),
        (owner_slot, smem),
    ]
    spaces = [anys, anys, anys, anys, vmem, vmem, anys, vmem, vmem]
    args += list(zip(tables(z), spaces))
    k, own, width, lay, tok = z.k, z.own, z.width, z.layer, z.tokens
    rows_all, unit = planes * tok, heads * tok
    half_rows = rd * CHUNKS
    two = 2 * slab

    def v(shape, dtype=F32):
        return pltpu.VMEM(shape, dtype)

    scratch = [
        v((ROWS, slab, flat), BF16), v(patch_w.shape, BF16), v((3, own, 256), BF16), v((own, 256), BF16),
        v((3 * PATCH * PATCH, k), BF16), v((32, 18 * 128), BF16), v((256, 7 * 64), BF16), v((384, 2 * k), BF16),
        v((z.pack, 3 * heads * 128), BF16),
        v((z.slab8, flat)), v((z.slab8, flat)), v((z.slab8, flat + 256), BF16), v((32, 128)),
        v((1152, 128), BF16), v((256, 896), BF16), v((CHUNKS * z.slab8, 128)),
        v((slab, 8, 384)), v((slab, 8, 384)), v((rd, 8, 384)), v((lay, half_rows, 384), BF16), v((half_rows, 384), BF16),
        v((two, 128)), v((rd, two, 128)), v((8, k)), v((rd, 8, k)),
        v((k, z.pack), BF16), v((rd, z.part, z.pack), BF16), v((k, z.pack), BF16), v((k, 3 * heads * 128), BF16),
        v((width, k), BF16), v((width, heads * 128), BF16), v((z.win, k + 128)), v((k, k)),
        v((rows_all, k), BF16), v((rows_all, k)), v((rows_all, 3 * heads * 128), BF16), v((planes, unit, unit)),
        v((z.prow, heads * 128)), v((z.prow, width)), v((lay, z.prow, width)), v((rows_all, 3 * heads * 128), BF16),
        v((planes, half_rows, 384), BF16), v((lay, half_rows, 384), BF16), v((rd, 8, 384)), v((rd, 8, 384)),
        v((7, z.slab8 * 8, 128)), v((two, 128)), v((rd, two, 128)),
        v((rows_all, 128)), v((z.prow, heads * 128)), v((z.prow, k)),
        pltpu.SemaphoreType.DMA((9,)),
    ]
    for copies in [rd - 1] * 7 + [lay - 1] * 3 + [rd - 1] * 2:
        scratch += [pltpu.SemaphoreType.DMA((copies,))] * 2
    grad, reward = pl.pallas_call(
        functools.partial(kernel, z, split_axes, split_sizes),
        out_shape=[
            jax.ShapeDtypeStruct((ROWS, slab, flat), BF16),
            jax.ShapeDtypeStruct((1, 1), F32),
        ],
        in_specs=[spec for _, spec in args],
        out_specs=[vmem, vmem],
        scratch_shapes=scratch,
        compiler_params=pltpu.CompilerParams(
            collective_id=0, has_side_effects=True, vmem_limit_bytes=58 * 2**20
        ),
    )(*[value for value, _ in args])
    return jnp.transpose(grad, (1, 0, 2)).reshape(slab, ROWS, 1, flat), reward.reshape(1)


def solution(mesh):
    placed = (
        P(("grp", "img"), "rows", "tp", None),
        P("tp"),
        P(None, None, None, "tp"),
        P("rows", None),
        P(),
        P(),
        P("rows", None, "tp"),
        P("rows", "tp"),
        P(),
        P(),
        P(("grp", "img"), None),
    )
    return jax.shard_map(
        body,
        mesh=mesh,
        in_specs=placed,
        out_specs=(P(("grp", "img"), "rows", "tp", None), P(("grp", "img", "rows"))),
        check_vma=False,
    )
```

```python
import functools
import math

import jax
import jax.numpy as jnp
import numpy as np
from jax import lax
from jax.experimental import pallas as pl
from jax.experimental.pallas import tpu as pltpu
from jax.sharding import PartitionSpec as P

C = 128
GROUPS = 32
PATCH = 14
HEAD_DIM = 80
W = 112
CHUNK = 14
CHUNKS = W // CHUNK
ROWS = 7
CELL = 160
CELL_USED = 147
EPS_GROUP = 1e-06
EPS_LAYER = 1e-05
F32 = jnp.float32
BF16 = jnp.bfloat16
EXACT = lax.Precision.HIGHEST


def up(count, step):
    return (count + step - 1) // step * step


def mm(left, right, left_dim=1, right_dim=0, precision=None):
    return lax.dot_general(
        left, right, (((left_dim,), (right_dim,)), ((), ())),
        preferred_element_type=F32, precision=precision,
    )


def split(values):
    high = values.astype(BF16)
    return high, (values - high.astype(F32)).astype(BF16)


class Sizes:
    def __init__(self, slab, rows_devices, planes, tp, width, span, heads, half_width):
        self.slab = slab
        self.rows_devices = rows_devices
        self.planes = planes
        self.tp = tp
        self.layer = planes * tp
        self.width = width
        self.span = span
        self.heads = heads
        self.half_width = half_width
        self.tokens = rows_devices * 2 * CHUNKS
        self.own = width // rows_devices
        self.ones = CELL + self.tokens
        self.k = up(up(self.ones + rows_devices, 16 * rows_devices), 256)
        self.part = self.k // rows_devices
        self.pack = up(3 * span, 128)
        self.win = up(min(self.own + 127, width), 128)
        self.slab8 = 8 * slab
        self.prow = up(planes, 8)
        self.mfold = 8 // planes if planes <= 4 else 1
        self.f_more = CELL_USED - 128
        self.f_groups = 128 // self.f_more
        while self.own % (16 * self.f_groups):
            self.f_groups -= 1
        self.f_rows = self.own + self.own // self.f_groups
        self.share = self.layer if self.f_rows % (16 * self.layer) == 0 else tp
        self.f_part = self.f_rows // self.share
        self.o_more = max(span - 128, 0)
        self.o_groups = 128 // self.o_more if self.o_more else 1
        self.o_rows = self.own + (self.own // self.o_groups if self.o_more else 0)


def tables(z):
    fold = np.zeros((3 * PATCH * PATCH, z.k), np.float32)
    for entry in range(3 * PATCH * PATCH):
        pixel, colour = divmod(entry, 3)
        row, col = divmod(pixel, PATCH)
        fold[entry, colour * 49 + row // 2 * 7 + col // 2] = 1
    place_f = np.zeros((32, 18 * 128), np.float32)
    place_b = np.zeros((256, 7 * 64), np.float32)
    for colour in range(3):
        for ky in range(3):
            for kx in range(3):
                tap = colour * 9 + ky * 3 + kx
                for xx in range(CHUNK):
                    lane = 42 * ky + 14 * colour + xx
                    place_f[tap, (xx + kx + 1) * 128 + lane] = 1
                    out = xx + kx - 1
                    if 0 <= out < CHUNK:
                        place_b[lane, out // 2 * 64 + out % 2 * 32 + tap] = 1
                if kx == 2:
                    place_b[128 + 42 * ky + 14 * colour + 13, tap] = 1
                if kx == 0:
                    place_b[128 + 42 * ky + 14 * colour, 6 * 64 + 32 + tap] = 1
    cell = np.zeros((384, 2 * z.k), np.float32)
    for half in range(2):
        for row in range(ROWS):
            for colour in range(3):
                for col in range(7):
                    line = row + 1
                    cell[line // 3 * 128 + line % 3 * 42 + colour * 14 + half * 7 + col,
                         half * z.k + colour * 49 + row * 7 + col] = 1
    rd = z.rows_devices
    hot = np.zeros((z.tokens, z.k), np.float32)
    for half in range(2):
        for r in range(rd):
            for c in range(CHUNKS):
                hot[half * rd * CHUNKS + r * CHUNKS + c, CELL + r * 2 * CHUNKS + 2 * c + half] = 1
    selpos = np.zeros((z.tokens, z.k), np.float32)
    selpos[np.arange(z.tokens), CELL + np.arange(z.tokens)] = 1
    pick = np.zeros((z.pack, 3 * z.heads * 128), np.float32)
    for which in range(3):
        for head in range(z.heads):
            for lane in range(HEAD_DIM):
                pick[which * z.span + head * HEAD_DIM + lane, (which * z.heads + head) * 128 + lane] = 1
    group = np.zeros((128, 128), np.float32)
    lanes = np.arange(128)
    group[lanes[:, None] % 64 // 4 == lanes[None, :] % 64 // 4] = 1
    rowsel = np.zeros((2 * z.slab, 2 * z.slab8), np.float32)
    for s in range(z.slab):
        for y in range(ROWS):
            rowsel[s, y * z.slab + s] = 1
            rowsel[z.slab + s, z.slab8 + y * z.slab + s] = 1
    bf = lambda a: jnp.asarray(a, BF16)
    return [bf(fold), bf(place_f), bf(place_b), bf(cell), bf(hot), bf(selpos), bf(pick),
            jnp.asarray(group, F32), jnp.asarray(rowsel, F32)]


class Sender:
    def __init__(self, sems):
        self.send, self.recv = sems
        self.copies = []

    def start(self, src, dst, where):
        at = len(self.copies)
        copy = pltpu.make_async_remote_copy(
            src_ref=src, dst_ref=dst, send_sem=self.send.at[at], recv_sem=self.recv.at[at],
            device_id=where, device_id_type=pl.DeviceIdType.MESH,
        )
        copy.start()
        self.copies.append(copy)

    def arrive(self):
        for copy in self.copies:
            copy.wait_recv()

    def finish(self):
        for copy in self.copies:
            copy.wait_send()


def kernel(
    z, split_axes, split_sizes,
    feat_hbm, gn_ref, conv_ref, patch_hbm, pos_ref, ln1_ref, qkv_hbm, out_hbm, fin_ref, head_ref, slot_ref,
    fold_hbm, placef_hbm, placeb_hbm, cell_hbm, hot_ref, selpos_ref, pick_hbm, group_ref, rowsel_ref,
    grad_ref, reward_ref,
    feat, patch, qkvw, outw, fold, placef, placeb, cell, pick,
    xs, slope, act, cwf, bandf, bandb, tmp_t, out1, sb1, p1, pics, pp,
    stat_own, stat_buf, mean_own, mean_buf, ypart, rsbuf, yfull, yh, eprime, owin, posw, dmat,
    fpack, fbuf, opack, obuf, ln1_row,
    aaug, am, qkv, prob, att, mx_own, mx, dqkv, dpart, dbuf, sb2, b1, dact, bs_own, bs_buf,
    invs, share, uk,
    local_sems, *remote,
):
    sems = [Sender(remote[2 * i : 2 * i + 2]) for i in range(len(remote) // 2)]
    s_stat, s_mean, s_rs, s_ag, s_e, s_o, s_1, s_2, s_mix, s_b2, s_b1, s_bst, s_f = sems
    rd, slab, tokens, k = z.rows_devices, z.slab, z.tokens, z.k
    planes, heads, span = z.planes, z.heads, z.span
    me = lax.axis_index("rows")
    plane = 0
    for axis, size in zip(split_axes, split_sizes):
        plane = plane * size + lax.axis_index(axis)
    tp = lax.axis_index("tp")
    lay = plane * z.tp + tp

    def column(offset):
        index = lax.rem(me + offset, rd)
        return index, {"rows": index}

    def neighbour(offset):
        index = lax.rem(lay + offset, z.layer)
        where = {"tp": lax.rem(index, z.tp)}
        rest = index // z.tp
        for axis, size in reversed(list(zip(split_axes, split_sizes))):
            where[axis] = lax.rem(rest, size)
            rest = rest // size
        return index, where

    def row(ref):
        return jnp.concatenate([ref[i : i + 1, :] for i in range(ref.shape[0])], axis=1)

    barrier = pltpu.get_barrier_semaphore()
    for offset in range(1, rd):
        pl.semaphore_signal(barrier, inc=1, device_id=column(offset)[1], device_id_type=pl.DeviceIdType.MESH)
    for offset in range(1, z.layer):
        pl.semaphore_signal(barrier, inc=1, device_id=neighbour(offset)[1], device_id_type=pl.DeviceIdType.MESH)

    start = jnp.minimum(plane * span // 128 * 128, z.half_width - 256)
    start = pl.multiple_of(start, 128)
    inside = plane * span - start
    window = pl.ds(start, 256)
    loads = []

    def load(src, dst):
        copy = pltpu.make_async_copy(src, dst, local_sems.at[len(loads)])
        copy.start()
        loads.append(copy)
        return copy

    l_feat = load(feat_hbm, feat)
    l_patch = load(patch_hbm, patch)
    l_fold = load(fold_hbm, fold)
    l_qkv = load(qkv_hbm.at[:, :, window], qkvw)
    l_pf = load(placef_hbm, placef)
    l_out = load(out_hbm.at[:, window], outw)
    l_pb = load(placeb_hbm, placeb)
    l_pick = load(pick_hbm, pick)
    l_cell = load(cell_hbm, cell)

    flat = CHUNKS * CHUNK * 64
    wide = CHUNK * 64
    used = ROWS * slab
    count = rd * ROWS * W * (C // GROUPS)

    def total_rows(first, second):
        return mm(rowsel_ref[...], jnp.concatenate([first, second], axis=0), precision=EXACT)

    def lanes_sum(values):
        total = values[:, 0:128]
        for block in range(1, values.shape[1] // 128):
            total = total + values[:, block * 128 : block * 128 + 128]
        return total

    l_feat.wait()
    xs[used:, :] = jnp.zeros((z.slab8 - used, flat), F32)
    for y in range(ROWS):
        xs[y * slab : y * slab + slab, :] = feat[y].astype(F32)

    def stats(c, carry):
        x = xs[:, pl.ds(pl.multiple_of(c * wide, 128), wide)]
        return carry[0] + lanes_sum(x), carry[1] + lanes_sum(x * x)

    zero = jnp.zeros((z.slab8, 128), F32)
    first, second = lax.fori_loop(0, CHUNKS, stats, (zero, zero))
    stat_own[...] = total_rows(first, second)
    pl.semaphore_wait(barrier, rd - 1 + z.layer - 1)
    for offset in range(1, rd):
        index, where = column(offset)
        s_stat.start(stat_own, stat_buf.at[me], where)
    stat_buf[me] = stat_own[...]

    begin = me * z.own
    wstart = jnp.minimum(begin // 128 * 128, z.width - z.win)
    wstart = pl.multiple_of(wstart, 128)
    wlanes = pl.ds(wstart, z.win)
    posw[:, :k] = mm(pos_ref[:, wlanes], selpos_ref[...], 0, 0)
    ln1_row[...] = row(ln1_ref)
    gains = jnp.broadcast_to(ln1_row[:, wlanes], (8, z.win)) * 0.125
    posw[:, k:] = mm(gains, jnp.ones((8, 128), F32), 0, 0, EXACT)
    own_rows = pl.ds(pl.multiple_of(begin - wstart, 16), z.own)
    l_patch.wait()
    l_fold.wait()
    e_own = mm(patch[...], fold[...]) + posw[own_rows, :k]
    mean = jnp.mean(e_own, axis=0, keepdims=True)
    mean_own[...] = jnp.broadcast_to(mean, (8, k))
    lane_k = lax.broadcasted_iota(jnp.int32, (1, k), 1)
    lane128 = lax.broadcasted_iota(jnp.int32, (1, 128), 1)
    e_own = e_own - mean + (lane_k == z.ones + me).astype(F32)
    gcol = posw[own_rows, k:]
    fpack[0 : z.own, :] = e_own[:, :128].astype(BF16)
    more = jnp.where(lane128 < z.f_more, e_own[:, 128:256], 0.0)
    each = z.own // z.f_groups
    packed = more[:each]
    for g in range(1, z.f_groups):
        packed = packed + pltpu.roll(more[g * each : g * each + each], g * z.f_more, 1)
    fpack[z.own :, :] = packed.astype(BF16)
    e_gain = (e_own * jnp.concatenate([gcol] * (k // 128), axis=1)).astype(BF16)
    l_qkv.wait()
    blocks = [jnp.zeros((k, 128), F32) for _ in range(z.pack // 128)]
    lane256 = lax.broadcasted_iota(jnp.int32, (1, 256), 1)
    for which in range(3):
        part = mm(e_gain, qkvw[which], 0, 0)
        base, off = divmod(span * which, 128)
        part = pltpu.roll(part, lax.rem(off - inside + 512, 256), 1)
        part = jnp.where((lane256 >= off) & (lane256 < off + span), part, 0.0)
        blocks[base] = blocks[base] + part[:, :128]
        if off + span > 128:
            blocks[base + 1] = blocks[base + 1] + part[:, 128:]
    ypart[...] = jnp.concatenate(blocks, axis=1).astype(BF16)

    def part_rows(index):
        return pl.ds(pl.multiple_of(index * z.part, 16), z.part)

    for offset in range(1, rd):
        index, where = column(offset)
        s_rs.start(ypart.at[part_rows(index)], rsbuf.at[me], where)
    rsbuf[me] = ypart[part_rows(me), :]
    for offset in range(1, rd):
        index, where = column(offset)
        s_mean.start(mean_own, mean_buf.at[me], where)
    mean_buf[me] = mean_own[...]
    share_me = lay if z.share == z.layer else tp
    f_mine = pl.ds(pl.multiple_of(share_me * z.f_part, 16), z.f_part)
    for offset in range(1, rd):
        index, where = column(offset)
        s_e.start(fpack.at[f_mine], fbuf.at[share_me, me], where)
    fbuf[share_me, me] = fpack[f_mine, :]
    l_out.wait()
    ow = pltpu.roll(outw[...].astype(F32), lax.rem(256 - inside, 256), 1)
    opack[0 : z.own, :] = ow[:, :128].astype(BF16)
    if z.o_more:
        each = z.own // z.o_groups
        more = jnp.where(lane128 < z.o_more, ow[:, 128:], 0.0)
        packed = more[:each]
        for g in range(1, z.o_groups):
            packed = packed + pltpu.roll(more[g * each : g * each + each], g * z.o_more, 1)
        opack[z.own :, :] = packed.astype(BF16)

    cwf[...] = jnp.zeros((32, 128), F32)
    for colour in range(3):
        for ky in range(3):
            cwf[pl.ds(9 * colour + 3 * ky, 3), 0:64] = conv_ref[colour, ky].astype(F32)
    taps = cwf[...]
    l_pf.wait()
    spread = mm(taps[:, :64].astype(BF16), placef[...], 0, 0).astype(BF16)
    for px in range(18):
        bandf[px * 64 : px * 64 + 64, :] = spread[:, px * 128 : px * 128 + 128]
    act[:, 0:128] = jnp.zeros((z.slab8, 128), BF16)
    act[:, 128 + flat :] = jnp.zeros((z.slab8, 128), BF16)

    s_stat.arrive()

    def tile(per_image):
        return jnp.concatenate([jnp.concatenate([per_image] * 8, axis=0)] * CHUNK_BLOCKS, axis=1)

    CHUNK_BLOCKS = wide // 128
    gain = jnp.concatenate([gn_ref[...], gn_ref[...]], axis=1)
    gain_wide = jnp.concatenate([gain] * CHUNK_BLOCKS, axis=1)

    def group_means(buf):
        total = buf[0]
        for r in range(1, rd):
            total = total + buf[r]
        return mm(total, group_ref[...], precision=EXACT) * (1.0 / count)

    both = group_means(stat_buf)
    average = both[:slab]
    inverse = lax.rsqrt(both[slab:] - average * average + EPS_GROUP)
    average_t = jnp.concatenate([average] * 8, axis=0)
    inverse_t = jnp.concatenate([inverse] * 8, axis=0)

    def activate(c, carry):
        at = pl.ds(pl.multiple_of(c * wide, 128), wide)
        x = xs[:, at]
        avg = jnp.concatenate([average_t] * CHUNK_BLOCKS, axis=1)
        inv = jnp.concatenate([inverse_t] * CHUNK_BLOCKS, axis=1)
        normed = (x - avg) * inv
        scaled = normed * gain_wide
        sig = 0.5 * jnp.tanh(0.5 * scaled) + 0.5
        xs[:, at] = normed
        active = scaled * sig
        act[:, pl.ds(pl.multiple_of(c * wide + 128, 128), wide)] = active.astype(BF16)
        slope[:, at] = sig * (1.0 + scaled - active) * gain_wide
        return carry

    lax.fori_loop(0, CHUNKS, activate, 0)
    lhs = jnp.concatenate([act[:, wide * c : wide * c + wide + 256] for c in range(CHUNKS)], axis=0)
    tmp_t[...] = mm(lhs, bandf[...])
    lane = lax.broadcasted_iota(jnp.int32, (8, 128), 1)

    def slot_mask(slot):
        return (lane >= 42 * slot) & (lane < 42 * slot + 42)

    masks = [slot_mask(j) for j in range(3)]

    def message(s, carry):
        acc = [jnp.zeros((8, 128), F32) for _ in range(3)]
        for y in range(ROWS):
            value = tmp_t[pl.ds(y * slab + s, 8, stride=z.slab8), :]
            for ky in range(3):
                block, j = divmod(y - ky + 2, 3)
                shift = 42 * (j - ky) % 128
                moved = value if shift == 0 else pltpu.roll(value, shift, 1)
                acc[block] = acc[block] + jnp.where(masks[j], moved, 0.0)
        out1[s] = jnp.concatenate(acc, axis=1)
        return carry

    for s in range(slab):
        message(s, 0)
    for slot in range(slab):
        source = 0
        for j in range(slab):
            source = jnp.where(slot_ref[0, j] == slot, j, source)
        sb1[slot] = out1[source]
    for offset in range(1, rd):
        index, where = column(offset)
        s_1.start(sb1.at[index], p1.at[me], where)
    p1[me] = sb1[me]

    s_e.arrive()
    for offset in range(1, z.share):
        where = neighbour(offset)[1] if z.share == z.layer else {"tp": lax.rem(tp + offset, z.tp)}
        s_f.start(fbuf.at[share_me], fbuf.at[share_me], where)
    s_rs.arrive()
    total = rsbuf[0].astype(F32)
    for r in range(1, rd):
        total = total + rsbuf[r].astype(F32)
    yfull[part_rows(me), :] = total.astype(BF16)
    for offset in range(1, rd):
        index, where = column(offset)
        s_ag.start(yfull.at[part_rows(me)], yfull.at[part_rows(me)], where)

    for offset in range(1, rd):
        index, where = column(offset)
        s_o.start(opack, obuf.at[me], where)
    obuf[me] = opack[...]
    l_pb.wait()
    tap64 = taps[:, :64]
    none = jnp.zeros((32, 64), F32)
    double = jnp.concatenate(
        [jnp.concatenate([tap64, none], axis=1), jnp.concatenate([none, tap64], axis=1)], axis=0
    ).astype(BF16)
    for pair in range(7):
        bandb[:, pair * 128 : pair * 128 + 128] = mm(
            placeb[:, pair * 64 : pair * 64 + 64], double
        ).astype(BF16)

    s_1.arrive()
    slabs = [p1[r] for r in range(rd)]
    keep = [lane >= 42, lane >= 0, lane < 84]
    for r in range(rd):
        parts = [jnp.where(keep[b], slabs[r][:, b * 128 : b * 128 + 128], 0.0) for b in range(3)]
        parts[1] = jnp.where(lane < 126, parts[1], 0.0)
        parts[0] = jnp.where(lane < 126, parts[0], 0.0)
        if r > 0:
            parts[0] = parts[0] + jnp.where(masks[1], pltpu.roll(slabs[r - 1][:, 256:384], 86, 1), 0.0)
        if r < rd - 1:
            parts[2] = parts[2] + jnp.where(masks[1], pltpu.roll(slabs[r + 1][:, 0:128], 42, 1), 0.0)
        tmp_t[pl.ds(r * 8, 8), :] = parts[0]
        tmp_t[pl.ds(rd * 8 + r * 8, 8), :] = parts[1]
        tmp_t[pl.ds(2 * rd * 8 + r * 8, 8), :] = parts[2]
    half_rows = rd * CHUNKS
    pp[...] = jnp.concatenate(
        [tmp_t[b * half_rows : b * half_rows + half_rows, :] for b in range(3)], axis=1
    ).astype(BF16)
    for offset in range(1, z.layer):
        index, where = neighbour(offset)
        s_2.start(pp, pics.at[lay], where)
    pics[lay] = pp[...]

    s_mean.arrive()
    dmat[...] = jnp.zeros((k, k), F32)
    middle = mean_buf[0][0:1]
    for r in range(1, rd):
        middle = middle + mean_buf[r][0:1]
    middle = middle * (1.0 / rd)
    for r in range(rd):
        dmat[z.ones + r : z.ones + r + 1, :] = mean_buf[r][0:1] - middle
    dm = dmat[...].astype(BF16)
    l_pick.wait()
    l_cell.wait()
    s_ag.arrive()
    yh[...] = mm(yfull[...], pick[...]).astype(BF16)
    s_f.arrive()
    each = z.own // z.f_groups
    for r in range(rd):
        block = slice(r * z.own, r * z.own + z.own)
        pos = mm(pos_ref[:, block], selpos_ref[...], 0, 0)
        pos = pos - jnp.mean(pos, axis=0, keepdims=True) + (lane_k == z.ones + r).astype(F32)
        packed = jnp.concatenate([fbuf[n, r] for n in range(z.share)], axis=0).astype(F32)
        more = jnp.concatenate(
            [
                jnp.where(lane128 < z.f_more, pltpu.roll(packed[z.own :], (128 - g * z.f_more) % 128, 1), 0.0)
                for g in range(z.f_groups)
            ],
            axis=0,
        )
        eprime[block, 0:128] = packed[: z.own].astype(BF16)
        eprime[block, 128:256] = (more + pos[:, 128:256]).astype(BF16)
        if k > 256:
            eprime[block, 256:] = pos[:, 256:].astype(BF16)
    gram_high, gram_low = split(mm(eprime[...], eprime[...], 0, 0))

    s_2.arrive()
    rows_all = planes * tokens
    picture = jnp.concatenate(
        [
            sum(pics[pi * z.tp + t].astype(F32) for t in range(z.tp)).astype(BF16)
            for pi in range(planes)
        ],
        axis=0,
    )
    halves = [mm(picture, cell[:, h * k : h * k + k]) for h in range(2)]
    hot = hot_ref[...].astype(F32)
    pieces = []
    for pi in range(planes):
        for h in range(2):
            pieces.append(
                halves[h][pi * half_rows : pi * half_rows + half_rows]
                + hot[h * half_rows : h * half_rows + half_rows]
            )
    cells = jnp.concatenate(pieces, axis=0)
    aug = (cells + mm(cells.astype(BF16), dm, 1, 1)).astype(BF16)
    aaug[...] = aug
    am[...] = mm(aug, gram_high) + mm(aug, gram_low)
    spread_in = jnp.sum(am[...] * aug.astype(F32), axis=1, keepdims=True) * (1.0 / z.width)
    inv_in = lax.rsqrt(jnp.maximum(spread_in, 0.0) + EPS_LAYER)
    invs[...] = jnp.broadcast_to(inv_in, (rows_all, 128))
    qkv[...] = (mm(aug, yh[...]) * inv_in).astype(BF16)

    unit = heads * tokens
    factor = 1.0 / math.sqrt(HEAD_DIM)
    row_u = lax.broadcasted_iota(jnp.int32, (unit, unit), 0)
    col_u = lax.broadcasted_iota(jnp.int32, (unit, unit), 1)
    same = row_u < 0
    for head in range(heads):
        low, high = head * tokens, head * tokens + tokens
        same = same | ((row_u >= low) & (row_u < high) & (col_u >= low) & (col_u < high))
    lane_u = lax.broadcasted_iota(jnp.int32, (1, unit), 1)

    def stacked(ref, pi, which):
        parts = [
            ref[pi * tokens : pi * tokens + tokens, (which * heads + h) * 128 : (which * heads + h) * 128 + 128]
            for h in range(heads)
        ]
        return jnp.concatenate(parts, axis=0) if heads > 1 else parts[0]

    for pi in range(planes):
        scores = mm(stacked(qkv, pi, 0), stacked(qkv, pi, 1), 1, 1) * factor
        if heads > 1:
            scores = jnp.where(same, scores, -1e30)
        top = jnp.max(scores, axis=1, keepdims=True)
        grown = jnp.exp(scores - top)
        soft = grown / jnp.sum(grown, axis=1, keepdims=True)
        prob[pi] = soft
        col_mean = jnp.sum(soft.astype(BF16).astype(F32), axis=0, keepdims=True) * (1.0 / tokens)
        per_head = jnp.concatenate(
            [
                jnp.where((lane_u >= h * tokens) & (lane_u < h * tokens + tokens), col_mean, 0.0)
                for h in range(heads)
            ]
            + [jnp.zeros((8 - heads, unit), F32)],
            axis=0,
        )
        high, low = split(per_head)
        value = stacked(qkv, pi, 2)
        result = mm(high, value) + mm(low, value)
        for h in range(heads):
            att[pi : pi + 1, h * 128 : h * 128 + 128] = result[h : h + 1]
    s_o.arrive()
    each = z.own // z.o_groups
    for r in range(rd):
        block = slice(r * z.own, r * z.own + z.own)
        main = obuf[r, 0 : z.own, :].astype(F32)
        for head in range(heads):
            low = head * HEAD_DIM
            first = max(min(HEAD_DIM, 128 - low), 0)
            moved = main if low == 0 else pltpu.roll(main, 128 - low, 1)
            moved = jnp.where(lane128 < first, moved, 0.0)
            if first < HEAD_DIM:
                extra = obuf[r, z.own :, :].astype(F32)
                moved = moved + jnp.concatenate(
                    [
                        jnp.where(
                            (lane128 >= first) & (lane128 < HEAD_DIM),
                            pltpu.roll(extra, (first - (low + first - 128) - g * z.o_more) % 128, 1),
                            0.0,
                        )
                        for g in range(z.o_groups)
                    ],
                    axis=0,
                )
            owin[block, head * 128 : head * 128 + 128] = moved.astype(BF16)
    if z.prow > planes:
        att[planes:, :] = jnp.zeros((z.prow - planes, heads * 128), F32)
    high, low = split(att[...])
    both = mm(jnp.concatenate([high, low], axis=0), owin[...], 1, 1)
    both = both[: z.prow] + both[z.prow :]
    part_width = z.width // z.mfold
    mx_own[...] = jnp.concatenate(
        [both[: 8 // z.mfold, f * part_width : f * part_width + part_width] for f in range(z.mfold)], axis=0
    )
    for offset in range(1, z.layer):
        index, where = neighbour(offset)
        s_mix.start(mx_own, mx.at[lay], where)
    mx[lay] = mx_own[...]
    means = [
        jnp.mean(aaug[pi * tokens : pi * tokens + tokens, :].astype(F32), axis=0, keepdims=True)
        for pi in range(planes)
    ]
    if z.prow > planes:
        means.append(jnp.zeros((z.prow - planes, k), F32))
    high, low = split(jnp.concatenate(means, axis=0))
    both = mm(jnp.concatenate([high, low], axis=0), eprime[...], 1, 1)
    pooled = both[: z.prow] + both[z.prow :]

    s_mix.arrive()
    mixed = mx[0]
    for index in range(1, z.layer):
        mixed = mixed + mx[index]
    if z.mfold > 1:
        mixed = jnp.concatenate([mixed[f * planes : f * planes + planes] for f in range(z.mfold)], axis=1)
        mixed = jnp.concatenate([mixed, jnp.zeros((z.prow - planes, z.width), F32)], axis=0)
    pooled = pooled + mixed
    final_gain, head_w = row(fin_ref), row(head_ref)
    centred = pooled - jnp.mean(pooled, axis=1, keepdims=True)
    inv_z = lax.rsqrt(jnp.mean(centred * centred, axis=1, keepdims=True) + EPS_LAYER)
    hat_z = centred * inv_z
    rewards = jnp.sum(hat_z * final_gain * head_w, axis=1, keepdims=True)
    mine = lax.broadcasted_iota(jnp.int32, (z.prow, 1), 0) == plane
    reward_ref[...] = jnp.sum(jnp.where(mine, rewards, 0.0), axis=0, keepdims=True)
    query = head_w * final_gain
    upstream = inv_z * (
        query - jnp.mean(query, axis=1, keepdims=True) - hat_z * jnp.mean(query * hat_z, axis=1, keepdims=True)
    )
    up16 = upstream.astype(BF16)
    share[...] = mm(up16, owin[...])
    uk[...] = mm(up16, eprime[...]) * (lay == 0).astype(F32)

    for pi in range(planes):
        q, key, value = (stacked(qkv, pi, which) for which in range(3))
        soft = prob[pi]
        parts = [
            jnp.broadcast_to(share[pi : pi + 1, h * 128 : h * 128 + 128], (tokens, 128)) for h in range(heads)
        ]
        given = (jnp.concatenate(parts, axis=0) if heads > 1 else parts[0]).astype(BF16)
        dprob = mm(given, value, 1, 1)
        dscores = (soft * (dprob - jnp.sum(dprob * soft, axis=1, keepdims=True)) * factor).astype(BF16)
        grads = [mm(dscores, key), mm(dscores, q, 0, 0), mm(soft.astype(BF16), given, 0, 0)]
        for which in range(3):
            for h in range(heads):
                dqkv[
                    pi * tokens : pi * tokens + tokens,
                    (which * heads + h) * 128 : (which * heads + h) * 128 + 128,
                ] = grads[which][h * tokens : h * tokens + tokens].astype(BF16)
    back = dqkv[...]
    inv_in = invs[:, 0:1]
    mean_two = jnp.sum(back.astype(F32) * qkv[...].astype(F32), axis=1, keepdims=True) * (1.0 / z.width)
    zk = inv_in * (mm(back, yh[...], 1, 1) - (mean_two * inv_in) * am[...])
    zk = zk + jnp.concatenate(
        [jnp.broadcast_to(uk[pi : pi + 1, :], (tokens, k)) for pi in range(planes)], axis=0
    )
    dcells = (zk + mm(zk.astype(BF16), dm)).astype(BF16)
    dpic = None
    for h in range(2):
        rows = jnp.concatenate(
            [dcells[pi * tokens + h * half_rows : pi * tokens + h * half_rows + half_rows] for pi in range(planes)],
            axis=0,
        )
        term = mm(rows, cell[:, h * k : h * k + k], 1, 1)
        dpic = term if dpic is None else dpic + term
    for pi in range(planes):
        dpart[pi] = dpic[pi * half_rows : pi * half_rows + half_rows].astype(BF16)
    for offset in range(1, z.layer):
        index, where = neighbour(offset)
        s_b2.start(dpart.at[index // z.tp], dbuf.at[lay], where)
    dbuf[lay] = dpart[plane]
    s_b2.arrive()
    total = dbuf[0].astype(F32)
    for index in range(1, z.layer):
        total = total + dbuf[index].astype(F32)
    total = total.astype(BF16).astype(F32)
    for r in range(rd):
        parts = [total[r * 8 : r * 8 + 8, b * 128 : b * 128 + 128] for b in range(3)]
        if r > 0:
            above = total[r * 8 - 8 : r * 8, 256:384]
            parts[0] = parts[0] + jnp.where(masks[0], pltpu.roll(above, 86, 1), 0.0)
        if r < rd - 1:
            below = total[r * 8 + 8 : r * 8 + 16, 0:128]
            parts[2] = parts[2] + jnp.where(masks[2], pltpu.roll(below, 42, 1), 0.0)
        sb2[r] = jnp.concatenate(parts, axis=1)
    for offset in range(1, rd):
        index, where = column(offset)
        s_b1.start(sb2.at[index], b1.at[me], where)
    b1[me] = sb2[me]
    s_b1.arrive()

    image_rows = slab * 8
    grads = jnp.concatenate([b1[slot_ref[0, j]] for j in range(slab)], axis=0)
    lane_s = lax.broadcasted_iota(jnp.int32, (image_rows, 128), 1)
    chunk_s = lax.rem(lax.broadcasted_iota(jnp.int32, (image_rows, 128), 0), 8)
    column_s = lax.rem(lane_s, CHUNK)
    from_left = (column_s == CHUNK - 1) & (chunk_s > 0)
    from_right = (column_s == 0) & (chunk_s < CHUNKS - 1)
    lines = []
    for y in range(ROWS):
        main = jnp.zeros((image_rows, 128), F32)
        for ky in range(3):
            block, j = divmod(y + 2 - ky, 3)
            shift = 42 * (ky - j) % 128
            moved = grads[:, block * 128 : block * 128 + 128]
            moved = moved if shift == 0 else pltpu.roll(moved, shift, 1)
            main = main + jnp.where((lane_s >= 42 * ky) & (lane_s < 42 * ky + 42), moved, 0.0)
        rim = jnp.where(from_left, pltpu.roll(main, 1, 0), 0.0)
        rim = jnp.where(from_right, pltpu.roll(main, image_rows - 1, 0), rim)
        lines.append(jnp.concatenate([main, rim], axis=1).astype(BF16))
    lines.append(jnp.zeros((image_rows, 256), BF16))
    lhs = jnp.concatenate(lines, axis=0)
    spread = mm(lhs, bandb[...])
    for block in range(CHUNK_BLOCKS):
        dact[block] = spread[:, block * 128 : block * 128 + 128]

    def gate(c, carry):
        at = pl.ds(pl.multiple_of(c * wide, 128), wide)
        parts = [
            dact[block, pl.ds(c, z.slab8, stride=8), :] for block in range(CHUNK_BLOCKS)
        ]
        gated = jnp.concatenate(parts, axis=1) * slope[:, at]
        slope[:, at] = gated
        return carry[0] + lanes_sum(gated), carry[1] + lanes_sum(gated * xs[:, at])

    first, second = lax.fori_loop(0, CHUNKS, gate, (zero, zero))
    bs_own[...] = total_rows(first, second)
    for offset in range(1, rd):
        index, where = column(offset)
        s_bst.start(bs_own, bs_buf.at[me], where)
    bs_buf[me] = bs_own[...]
    s_bst.arrive()
    both = group_means(bs_buf)
    one_t = jnp.concatenate([both[:slab]] * 8, axis=0)
    two_t = jnp.concatenate([both[slab:]] * 8, axis=0)

    def finish(c, carry):
        at = pl.ds(pl.multiple_of(c * wide, 128), wide)
        one = jnp.concatenate([one_t] * CHUNK_BLOCKS, axis=1)
        two = jnp.concatenate([two_t] * CHUNK_BLOCKS, axis=1)
        inv = jnp.concatenate([inverse_t] * CHUNK_BLOCKS, axis=1)
        value = inv * (slope[:, at] - one - xs[:, at] * two)
        for y in range(ROWS):
            grad_ref[y, :, at] = value[y * slab : y * slab + slab].astype(BF16)
        return carry

    lax.fori_loop(0, CHUNKS, finish, 0)
    for sender in sems:
        sender.finish()


def body(features, gn_gain, conv_w, patch_w, pos_emb, ln1_gain, qkv_w, out_w, final_gain, head_w, owner_slot):
    slab = features.shape[0]
    rd = lax.axis_size("rows")
    tp = lax.axis_size("tp")
    half_width = qkv_w.shape[2]
    heads_half = half_width // HEAD_DIM
    split_axes = ("grp", "img")
    if heads_half % (lax.axis_size("grp") * lax.axis_size("img")):
        split_axes = ("img",)
    split_sizes = tuple(lax.axis_size(axis) for axis in split_axes)
    planes = math.prod(split_sizes)
    heads = heads_half // planes
    z = Sizes(slab, rd, planes, tp, pos_emb.shape[1], heads * HEAD_DIM, heads, half_width)
    flat = features.shape[3]
    vmem = pl.BlockSpec(memory_space=pltpu.VMEM)
    anys = pl.BlockSpec(memory_space=pl.ANY)
    smem = pl.BlockSpec(memory_space=pltpu.SMEM)
    args = [
        (jnp.transpose(features.reshape(slab, ROWS, flat), (1, 0, 2)), anys),
        (gn_gain.reshape(1, -1), vmem),
        (conv_w, vmem),
        (patch_w, anys),
        (pos_emb, vmem),
        (ln1_gain.reshape(-1, 128), vmem),
        (jnp.transpose(qkv_w, (1, 0, 2)), anys),
        (out_w, anys),
        (final_gain.reshape(-1, 128), vmem),
        (head_w.reshape(-1, 128), vmem),
        (owner_slot, smem),
    ]
    spaces = [anys, anys, anys, anys, vmem, vmem, anys, vmem, vmem]
    args += list(zip(tables(z), spaces))
    k, own, width, lay, tok = z.k, z.own, z.width, z.layer, z.tokens
    rows_all, unit = planes * tok, heads * tok
    half_rows = rd * CHUNKS
    two = 2 * slab

    def v(shape, dtype=F32):
        return pltpu.VMEM(shape, dtype)

    scratch = [
        v((ROWS, slab, flat), BF16), v(patch_w.shape, BF16), v((3, own, 256), BF16), v((own, 256), BF16),
        v((3 * PATCH * PATCH, k), BF16), v((32, 18 * 128), BF16), v((256, 7 * 64), BF16), v((384, 2 * k), BF16),
        v((z.pack, 3 * heads * 128), BF16),
        v((z.slab8, flat)), v((z.slab8, flat)), v((z.slab8, flat + 256), BF16), v((32, 128)),
        v((1152, 128), BF16), v((256, 896), BF16), v((CHUNKS * z.slab8, 128)),
        v((slab, 8, 384)), v((slab, 8, 384)), v((rd, 8, 384)), v((lay, half_rows, 384), BF16), v((half_rows, 384), BF16),
        v((two, 128)), v((rd, two, 128)), v((8, k)), v((rd, 8, k)),
        v((k, z.pack), BF16), v((rd, z.part, z.pack), BF16), v((k, z.pack), BF16), v((k, 3 * heads * 128), BF16),
        v((width, k), BF16), v((width, heads * 128), BF16), v((z.win, k + 128)), v((k, k)),
        v((z.f_rows, 128), BF16), v((z.share, rd, z.f_part, 128), BF16), v((z.o_rows, 128), BF16), v((rd, z.o_rows, 128), BF16),
        v((1, width)),
        v((rows_all, k), BF16), v((rows_all, k)), v((rows_all, 3 * heads * 128), BF16), v((planes, unit, unit)),
        v((z.prow, heads * 128)), v((8, width // z.mfold)), v((lay, 8, width // z.mfold)), v((rows_all, 3 * heads * 128), BF16),
        v((planes, half_rows, 384), BF16), v((lay, half_rows, 384), BF16), v((rd, 8, 384)), v((rd, 8, 384)),
        v((7, z.slab8 * 8, 128)), v((two, 128)), v((rd, two, 128)),
        v((rows_all, 128)), v((z.prow, heads * 128)), v((z.prow, k)),
        pltpu.SemaphoreType.DMA((9,)),
    ]
    for copies in [rd - 1] * 7 + [lay - 1] * 3 + [rd - 1] * 2 + [z.share - 1]:
        scratch += [pltpu.SemaphoreType.DMA((copies,))] * 2
    grad, reward = pl.pallas_call(
        functools.partial(kernel, z, split_axes, split_sizes),
        out_shape=[
            jax.ShapeDtypeStruct((ROWS, slab, flat), BF16),
            jax.ShapeDtypeStruct((1, 1), F32),
        ],
        in_specs=[spec for _, spec in args],
        out_specs=[vmem, vmem],
        scratch_shapes=scratch,
        compiler_params=pltpu.CompilerParams(
            collective_id=0, has_side_effects=True, vmem_limit_bytes=58 * 2**20
        ),
    )(*[value for value, _ in args])
    return jnp.transpose(grad, (1, 0, 2)).reshape(slab, ROWS, 1, flat), reward.reshape(1)


def solution(mesh):
    placed = (
        P(("grp", "img"), "rows", "tp", None),
        P("tp"),
        P(None, None, None, "tp"),
        P("rows", None),
        P(),
        P(),
        P("rows", None, "tp"),
        P("rows", "tp"),
        P(),
        P(),
        P(("grp", "img"), None),
    )
    return jax.shard_map(
        body,
        mesh=mesh,
        in_specs=placed,
        out_specs=(P(("grp", "img"), "rows", "tp", None), P(("grp", "img", "rows"))),
        check_vma=False,
    )
```

```python
import functools
import math

import jax
import jax.numpy as jnp
import numpy as np
from jax import lax
from jax.experimental import pallas as pl
from jax.experimental.pallas import tpu as pltpu
from jax.sharding import PartitionSpec as P

C = 128
GROUPS = 32
PATCH = 14
HEAD_DIM = 80
W = 112
CHUNK = 14
CHUNKS = W // CHUNK
ROWS = 7
CELL = 152
CELL_USED = 147
EPS_GROUP = 1e-06
EPS_LAYER = 1e-05
F32 = jnp.float32
BF16 = jnp.bfloat16
EXACT = lax.Precision.HIGHEST


def up(count, step):
    return (count + step - 1) // step * step


def mm(left, right, left_dim=1, right_dim=0, precision=None):
    return lax.dot_general(
        left, right, (((left_dim,), (right_dim,)), ((), ())),
        preferred_element_type=F32, precision=precision,
    )


def split(values):
    high = values.astype(BF16)
    return high, (values - high.astype(F32)).astype(BF16)


class Sizes:
    def __init__(self, slab, rows_devices, planes, tp, width, span, heads, half_width):
        self.slab = slab
        self.rows_devices = rows_devices
        self.planes = planes
        self.tp = tp
        self.layer = planes * tp
        self.width = width
        self.span = span
        self.heads = heads
        self.half_width = half_width
        self.tokens = rows_devices * 2 * CHUNKS
        self.own = width // rows_devices
        self.ones = CELL + self.tokens
        self.k = up(up(self.ones + rows_devices, 32 * rows_devices), 256)
        self.pack = up(3 * span, 128)
        self.by_lanes = self.pack == 128 * rows_devices
        if self.by_lanes:
            self.chunk = (up(self.ones + rows_devices, 32) // 2, 128)
        else:
            self.chunk = (self.k // rows_devices // 2, self.pack)
        self.win = up(min(self.own + 127, width), 128)
        self.slab8 = 8 * slab
        self.prow = up(planes, 8)
        self.mfold = 8 // planes if planes <= 4 else 1
        self.mrows = up(width // self.mfold // 128 * 8, 16)
        self.f_more = CELL_USED - 128
        self.f_groups = 128 // self.f_more
        while self.own % (16 * self.f_groups):
            self.f_groups -= 1
        self.f_rows = self.own + self.own // self.f_groups
        self.share = self.layer if self.f_rows % (16 * self.layer) == 0 else tp
        self.f_part = self.f_rows // self.share
        self.o_more = max(span - 128, 0)
        self.o_groups = 128 // self.o_more if self.o_more else 1
        self.o_rows = self.own + (self.own // self.o_groups if self.o_more else 0)


def tables(z):
    fold = np.zeros((3 * PATCH * PATCH, z.k), np.float32)
    for entry in range(3 * PATCH * PATCH):
        pixel, colour = divmod(entry, 3)
        row, col = divmod(pixel, PATCH)
        fold[entry, colour * 49 + row // 2 * 7 + col // 2] = 1
    place_f = np.zeros((32, 18 * 128), np.float32)
    place_b = np.zeros((256, 7 * 64), np.float32)
    for colour in range(3):
        for ky in range(3):
            for kx in range(3):
                tap = colour * 9 + ky * 3 + kx
                for xx in range(CHUNK):
                    lane = 42 * ky + 14 * colour + xx
                    place_f[tap, (xx + kx + 1) * 128 + lane] = 1
                    out = xx + kx - 1
                    if 0 <= out < CHUNK:
                        place_b[lane, out // 2 * 64 + out % 2 * 32 + tap] = 1
                if kx == 2:
                    place_b[128 + 42 * ky + 14 * colour + 13, tap] = 1
                if kx == 0:
                    place_b[128 + 42 * ky + 14 * colour, 6 * 64 + 32 + tap] = 1
    cell = np.zeros((384, 2 * z.k), np.float32)
    for half in range(2):
        for row in range(ROWS):
            for colour in range(3):
                for col in range(7):
                    line = row + 1
                    cell[line // 3 * 128 + line % 3 * 42 + colour * 14 + half * 7 + col,
                         half * z.k + colour * 49 + row * 7 + col] = 1
    rd = z.rows_devices
    hot = np.zeros((z.tokens, z.k), np.float32)
    for half in range(2):
        for r in range(rd):
            for c in range(CHUNKS):
                hot[half * rd * CHUNKS + r * CHUNKS + c, CELL + r * 2 * CHUNKS + 2 * c + half] = 1
    selpos = np.zeros((z.tokens, z.k), np.float32)
    selpos[np.arange(z.tokens), CELL + np.arange(z.tokens)] = 1
    pick = np.zeros((z.pack, 3 * z.heads * 128), np.float32)
    for which in range(3):
        for head in range(z.heads):
            for lane in range(HEAD_DIM):
                pick[which * z.span + head * HEAD_DIM + lane, (which * z.heads + head) * 128 + lane] = 1
    group = np.zeros((128, 128), np.float32)
    lanes = np.arange(128)
    group[lanes[:, None] % 64 // 4 == lanes[None, :] % 64 // 4] = 1
    rowsel = np.zeros((2 * z.slab, 2 * z.slab8), np.float32)
    for s in range(z.slab):
        for y in range(ROWS):
            rowsel[s, y * z.slab + s] = 1
            rowsel[z.slab + s, z.slab8 + y * z.slab + s] = 1
    bf = lambda a: jnp.asarray(a, BF16)
    return [bf(fold), bf(place_f), bf(place_b), bf(cell), bf(hot), bf(selpos), bf(pick),
            jnp.asarray(group, F32), jnp.asarray(rowsel, F32)]


class Sender:
    def __init__(self, sems):
        self.send, self.recv = sems
        self.copies = []

    def start(self, src, dst, where):
        at = len(self.copies)
        copy = pltpu.make_async_remote_copy(
            src_ref=src, dst_ref=dst, send_sem=self.send.at[at], recv_sem=self.recv.at[at],
            device_id=where, device_id_type=pl.DeviceIdType.MESH,
        )
        copy.start()
        self.copies.append(copy)

    def arrive(self):
        for copy in self.copies:
            copy.wait_recv()

    def finish(self):
        for copy in self.copies:
            copy.wait_send()


def kernel(
    z, split_axes, split_sizes,
    feat_hbm, gn_hbm, conv_hbm, patch_hbm, pos_hbm, ln1_hbm, qkv_hbm, out_hbm, fin_hbm, head_hbm, slot_ref,
    fold_hbm, placef_hbm, placeb_hbm, cell_hbm, hot_hbm, selpos_hbm, pick_hbm, group_hbm, rowsel_hbm,
    grad_ref, reward_ref,
    feat, patch, qkvw, outw, fold, placef, placeb, cell, pick,
    gn_ref, conv_ref, pos_ref, ln1_ref, fin_ref, head_ref, hot_ref, selpos_ref, group_ref, rowsel_ref,
    xs, slope, act, cwf, bandf, bandb, tmp_t, out1, sb1, p1, pics, pp,
    stat_own, stat_buf, mean_own, mean_buf, ypart, rsbuf, yfull, yh, eprime, owin, posw, dmat,
    fpack, fbuf, opack, obuf, ln1_row,
    aaug, am, qkv, prob, att, mx_own, mx, dqkv, dpart, dbuf, sb2, b1, dact, bs_own, bs_buf,
    invs, share, uk,
    local_sems, *remote,
):
    sems = [Sender(remote[2 * i : 2 * i + 2]) for i in range(len(remote) // 2)]
    s_stat, s_mean, s_rs, s_ag, s_e, s_o, s_1, s_2, s_mix, s_b2, s_b1, s_bst, s_f, s_rs2, s_ag2, s_c = sems
    rd, slab, tokens, k = z.rows_devices, z.slab, z.tokens, z.k
    planes, heads, span = z.planes, z.heads, z.span
    me = lax.axis_index("rows")
    plane = 0
    for axis, size in zip(split_axes, split_sizes):
        plane = plane * size + lax.axis_index(axis)
    tp = lax.axis_index("tp")
    lay = plane * z.tp + tp

    def column(offset):
        index = lax.rem(me + offset, rd)
        return index, {"rows": index}

    def place(rest, where):
        for axis, size in reversed(list(zip(split_axes, split_sizes))):
            where[axis] = lax.rem(rest, size)
            rest = rest // size
        return where

    def neighbour(offset):
        index = lax.rem(lay + offset, z.layer)
        return index, place(index // z.tp, {"tp": lax.rem(index, z.tp)})

    def fellow(offset):
        index = lax.rem(plane + offset, planes)
        return index, place(index, {})

    def row(ref):
        return jnp.concatenate([ref[i : i + 1, :] for i in range(ref.shape[0])], axis=1)

    start = jnp.minimum(plane * span // 128 * 128, z.half_width - 256)
    start = pl.multiple_of(start, 128)
    inside = plane * span - start
    window = pl.ds(start, 256)
    loads = []

    def load(src, dst):
        copy = pltpu.make_async_copy(src, dst, local_sems.at[len(loads)])
        copy.start()
        loads.append(copy)
        return copy

    l_feat = load(feat_hbm, feat)
    l_rowsel = load(rowsel_hbm, rowsel_ref)

    barrier = pltpu.get_barrier_semaphore()
    for offset in range(1, rd):
        pl.semaphore_signal(barrier, inc=1, device_id=column(offset)[1], device_id_type=pl.DeviceIdType.MESH)
    for offset in range(1, z.layer):
        pl.semaphore_signal(barrier, inc=1, device_id=neighbour(offset)[1], device_id_type=pl.DeviceIdType.MESH)

    l_pos = load(pos_hbm, pos_ref)
    l_selpos = load(selpos_hbm, selpos_ref)
    l_ln1 = load(ln1_hbm, ln1_ref)
    l_patch = load(patch_hbm, patch)
    l_fold = load(fold_hbm, fold)
    l_qkv = load(qkv_hbm.at[:, :, window], qkvw)
    l_out = load(out_hbm.at[:, window], outw)
    l_conv = load(conv_hbm, conv_ref)
    l_pf = load(placef_hbm, placef)
    l_pb = load(placeb_hbm, placeb)
    l_group = load(group_hbm, group_ref)
    l_gn = load(gn_hbm, gn_ref)
    l_pick = load(pick_hbm, pick)
    l_cell = load(cell_hbm, cell)
    l_hot = load(hot_hbm, hot_ref)
    l_fin = load(fin_hbm, fin_ref)
    l_head = load(head_hbm, head_ref)

    flat = CHUNKS * CHUNK * 64
    wide = CHUNK * 64
    used = ROWS * slab
    count = rd * ROWS * W * (C // GROUPS)

    def total_rows(first, second):
        return mm(rowsel_ref[...], jnp.concatenate([first, second], axis=0), precision=EXACT)

    def lanes_sum(values):
        total = values[:, 0:128]
        for block in range(1, values.shape[1] // 128):
            total = total + values[:, block * 128 : block * 128 + 128]
        return total

    l_feat.wait()
    xs[used:, :] = jnp.zeros((z.slab8 - used, flat), F32)
    for y in range(ROWS):
        xs[y * slab : y * slab + slab, :] = feat[y].astype(F32)

    def stats(c, carry):
        x = xs[:, pl.ds(pl.multiple_of(c * wide, 128), wide)]
        return carry[0] + lanes_sum(x), carry[1] + lanes_sum(x * x)

    zero = jnp.zeros((z.slab8, 128), F32)
    first, second = lax.fori_loop(0, CHUNKS, stats, (zero, zero))
    l_rowsel.wait()
    stat_own[...] = total_rows(first, second)
    pl.semaphore_wait(barrier, rd - 1 + z.layer - 1)
    for offset in range(1, rd):
        index, where = column(offset)
        s_stat.start(stat_own, stat_buf.at[me], where)
    stat_buf[me] = stat_own[...]

    begin = me * z.own
    l_pos.wait()
    l_selpos.wait()
    l_ln1.wait()
    wstart = jnp.minimum(begin // 128 * 128, z.width - z.win)
    wstart = pl.multiple_of(wstart, 128)
    wlanes = pl.ds(wstart, z.win)
    posw[:, :k] = mm(pos_ref[:, wlanes], selpos_ref[...], 0, 0)
    ln1_row[...] = row(ln1_ref)
    gains = jnp.broadcast_to(ln1_row[:, wlanes], (8, z.win)) * 0.125
    posw[:, k:] = mm(gains, jnp.ones((8, 128), F32), 0, 0, EXACT)
    own_rows = pl.ds(pl.multiple_of(begin - wstart, 16), z.own)
    l_patch.wait()
    l_fold.wait()
    e_own = mm(patch[...], fold[...]) + posw[own_rows, :k]
    mean = jnp.mean(e_own, axis=0, keepdims=True)
    mean_own[...] = jnp.zeros((8, 128), F32)
    for block in range(k // 128):
        mean_own[block : block + 1, :] = mean[:, block * 128 : block * 128 + 128]
    lane_k = lax.broadcasted_iota(jnp.int32, (1, k), 1)
    lane128 = lax.broadcasted_iota(jnp.int32, (1, 128), 1)
    e_own = e_own - mean + (lane_k == z.ones + me).astype(F32)
    gcol = posw[own_rows, k:]
    fpack[0 : z.own, :] = e_own[:, :128].astype(BF16)
    more = jnp.where(lane128 < z.f_more, e_own[:, 128:256], 0.0)
    each = z.own // z.f_groups
    packed = more[:each]
    for g in range(1, z.f_groups):
        packed = packed + pltpu.roll(more[g * each : g * each + each], g * z.f_more, 1)
    fpack[z.own :, :] = packed.astype(BF16)
    e_gain = (e_own * jnp.concatenate([gcol] * (k // 128), axis=1)).astype(BF16)
    l_qkv.wait()
    blocks = [jnp.zeros((k, 128), F32) for _ in range(z.pack // 128)]
    lane256 = lax.broadcasted_iota(jnp.int32, (1, 256), 1)
    for which in range(3):
        part = mm(e_gain, qkvw[which], 0, 0)
        base, off = divmod(span * which, 128)
        part = pltpu.roll(part, lax.rem(off - inside + 512, 256), 1)
        part = jnp.where((lane256 >= off) & (lane256 < off + span), part, 0.0)
        blocks[base] = blocks[base] + part[:, :128]
        if off + span > 128:
            blocks[base + 1] = blocks[base + 1] + part[:, 128:]
    ypart[...] = jnp.concatenate(blocks, axis=1).astype(BF16)

    def part_of(index, half):
        tall = z.chunk[0]
        if z.by_lanes:
            return pl.ds(half * tall, tall), pl.ds(pl.multiple_of(index * 128, 128), 128)
        return pl.ds(pl.multiple_of((2 * index + half) * tall, 16), tall), slice(None)

    share_me = tp * planes + plane if z.share == z.layer else tp
    f_mine = pl.ds(pl.multiple_of(share_me * z.f_part, 16), z.f_part)
    for offset in range(1, rd):
        index, where = column(offset)
        s_e.start(fpack.at[f_mine], fbuf.at[share_me, me], where)
    fbuf[share_me, me] = fpack[f_mine, :]
    for half, sender in enumerate((s_rs, s_rs2)):
        for offset in range(1, rd):
            index, where = column(offset)
            sender.start(ypart.at[part_of(index, half)], rsbuf.at[half, me], where)
        rsbuf[half, me] = ypart[part_of(me, half)]
    for offset in range(1, rd):
        index, where = column(offset)
        s_mean.start(mean_own, mean_buf.at[me], where)
    mean_buf[me] = mean_own[...]
    l_conv.wait()
    cwf[...] = jnp.zeros((32, 128), F32)
    for colour in range(3):
        for ky in range(3):
            cwf[pl.ds(9 * colour + 3 * ky, 3), 0:64] = conv_ref[colour, ky].astype(F32)
    taps = cwf[...]
    l_pf.wait()
    spread = mm(taps[:, :64].astype(BF16), placef[...], 0, 0).astype(BF16)
    for px in range(18):
        bandf[px * 64 : px * 64 + 64, :] = spread[:, px * 128 : px * 128 + 128]
    act[:, 0:128] = jnp.zeros((z.slab8, 128), BF16)
    act[:, 128 + flat :] = jnp.zeros((z.slab8, 128), BF16)

    l_group.wait()
    l_gn.wait()
    s_stat.arrive()

    def tile(per_image):
        return jnp.concatenate([jnp.concatenate([per_image] * 8, axis=0)] * CHUNK_BLOCKS, axis=1)

    CHUNK_BLOCKS = wide // 128
    gain = jnp.concatenate([gn_ref[...], gn_ref[...]], axis=1)
    gain_wide = jnp.concatenate([gain] * CHUNK_BLOCKS, axis=1)

    def group_means(buf):
        total = buf[0]
        for r in range(1, rd):
            total = total + buf[r]
        return mm(total, group_ref[...], precision=EXACT) * (1.0 / count)

    both = group_means(stat_buf)
    average = both[:slab]
    inverse = lax.rsqrt(both[slab:] - average * average + EPS_GROUP)
    average_t = jnp.concatenate([average] * 8, axis=0)
    inverse_t = jnp.concatenate([inverse] * 8, axis=0)

    def activate(c, carry):
        at = pl.ds(pl.multiple_of(c * wide, 128), wide)
        x = xs[:, at]
        avg = jnp.concatenate([average_t] * CHUNK_BLOCKS, axis=1)
        inv = jnp.concatenate([inverse_t] * CHUNK_BLOCKS, axis=1)
        normed = (x - avg) * inv
        scaled = normed * gain_wide
        sig = 0.5 * jnp.tanh(0.5 * scaled) + 0.5
        xs[:, at] = normed
        active = scaled * sig
        act[:, pl.ds(pl.multiple_of(c * wide + 128, 128), wide)] = active.astype(BF16)
        slope[:, at] = sig * (1.0 + scaled - active) * gain_wide
        return carry

    lax.fori_loop(0, CHUNKS, activate, 0)
    lhs = jnp.concatenate([act[:, wide * c : wide * c + wide + 256] for c in range(CHUNKS)], axis=0)
    tmp_t[...] = mm(lhs, bandf[...])
    lane = lax.broadcasted_iota(jnp.int32, (8, 128), 1)

    def slot_mask(slot):
        return (lane >= 42 * slot) & (lane < 42 * slot + 42)

    masks = [slot_mask(j) for j in range(3)]

    def message(s, carry):
        acc = [jnp.zeros((8, 128), F32) for _ in range(3)]
        for y in range(ROWS):
            value = tmp_t[pl.ds(y * slab + s, 8, stride=z.slab8), :]
            for ky in range(3):
                block, j = divmod(y - ky + 2, 3)
                shift = 42 * (j - ky) % 128
                moved = value if shift == 0 else pltpu.roll(value, shift, 1)
                acc[block] = acc[block] + jnp.where(masks[j], moved, 0.0)
        out1[s] = jnp.concatenate(acc, axis=1)
        return carry

    for s in range(slab):
        message(s, 0)
    for slot in range(slab):
        source = 0
        for j in range(slab):
            source = jnp.where(slot_ref[0, j] == slot, j, source)
        sb1[slot] = out1[source]
    for offset in range(1, rd):
        index, where = column(offset)
        s_1.start(sb1.at[index], p1.at[me], where)
    p1[me] = sb1[me]

    def pack_out():
        l_out.wait()
        ow = pltpu.roll(outw[...].astype(F32), lax.rem(256 - inside, 256), 1)
        opack[0 : z.own, :] = ow[:, :128].astype(BF16)
        if z.o_more:
            each = z.own // z.o_groups
            more = jnp.where(lane128 < z.o_more, ow[:, 128:], 0.0)
            packed = more[:each]
            for g in range(1, z.o_groups):
                packed = packed + pltpu.roll(more[g * each : g * each + each], g * z.o_more, 1)
            opack[z.own :, :] = packed.astype(BF16)

    def taps_back():
        l_pb.wait()
        tap64 = taps[:, :64]
        none = jnp.zeros((32, 64), F32)
        double = jnp.concatenate(
            [jnp.concatenate([tap64, none], axis=1), jnp.concatenate([none, tap64], axis=1)], axis=0
        ).astype(BF16)
        for pair in range(7):
            bandb[:, pair * 128 : pair * 128 + 128] = mm(
                placeb[:, pair * 64 : pair * 64 + 64], double
            ).astype(BF16)
        for r in range(rd):
            block = slice(r * z.own, r * z.own + z.own)
            pos = mm(pos_ref[:, block], selpos_ref[...], 0, 0)
            pos = pos - jnp.mean(pos, axis=0, keepdims=True) + (lane_k == z.ones + r).astype(F32)
            eprime[block, 128:] = pos[:, 128:].astype(BF16)

    if z.by_lanes and 2 * z.chunk[0] < k:
        yfull[2 * z.chunk[0] :, :] = jnp.zeros((k - 2 * z.chunk[0], z.pack), BF16)
    s_e.arrive()
    if z.share == z.layer:
        for offset in range(1, planes):
            index, where = fellow(offset)
            s_f.start(fbuf.at[share_me], fbuf.at[share_me], where)
    for half, (sender, after) in enumerate(((s_rs, s_ag), (s_rs2, s_ag2))):
        sender.arrive()
        total = rsbuf[half, 0].astype(F32)
        for r in range(1, rd):
            total = total + rsbuf[half, r].astype(F32)
        yfull[part_of(me, half)] = total.astype(BF16)
        for offset in range(1, rd):
            index, where = column(offset)
            after.start(yfull.at[part_of(me, half)], yfull.at[part_of(me, half)], where)
        if half == 0:
            pack_out()
            taps_back()
    for offset in range(1, rd):
        index, where = column(offset)
        s_o.start(opack, obuf.at[me], where)
    obuf[me] = opack[...]
    s_1.arrive()
    slabs = [p1[r] for r in range(rd)]
    keep = [lane >= 42, lane >= 0, lane < 84]
    for r in range(rd):
        parts = [jnp.where(keep[b], slabs[r][:, b * 128 : b * 128 + 128], 0.0) for b in range(3)]
        parts[1] = jnp.where(lane < 126, parts[1], 0.0)
        parts[0] = jnp.where(lane < 126, parts[0], 0.0)
        if r > 0:
            parts[0] = parts[0] + jnp.where(masks[1], pltpu.roll(slabs[r - 1][:, 256:384], 86, 1), 0.0)
        if r < rd - 1:
            parts[2] = parts[2] + jnp.where(masks[1], pltpu.roll(slabs[r + 1][:, 0:128], 42, 1), 0.0)
        tmp_t[pl.ds(r * 8, 8), :] = parts[0]
        tmp_t[pl.ds(rd * 8 + r * 8, 8), :] = parts[1]
        tmp_t[pl.ds(2 * rd * 8 + r * 8, 8), :] = parts[2]
    half_rows = rd * CHUNKS
    pp[...] = jnp.concatenate(
        [tmp_t[b * half_rows : b * half_rows + half_rows, :] for b in range(3)], axis=1
    ).astype(BF16)
    for offset in range(1, z.layer):
        index, where = neighbour(offset)
        s_2.start(pp, pics.at[lay], where)
    pics[lay] = pp[...]

    s_f.arrive()
    group_size = z.share // z.tp
    group = fbuf.at[pl.ds(tp * group_size, group_size)]
    for offset in range(1, z.tp):
        s_c.start(group, group, {"tp": lax.rem(tp + offset, z.tp)})
    s_mean.arrive()
    dmat[...] = jnp.zeros((k, k), F32)
    block_means = [
        jnp.concatenate([mean_buf[r, block : block + 1, :] for block in range(k // 128)], axis=1) for r in range(rd)
    ]
    middle = sum(block_means) * (1.0 / rd)
    for r in range(rd):
        dmat[z.ones + r : z.ones + r + 1, :] = block_means[r] - middle
    dm = dmat[...].astype(BF16)
    l_pick.wait()
    l_cell.wait()
    s_ag.arrive()
    s_ag2.arrive()
    yh[...] = mm(yfull[...], pick[...]).astype(BF16)
    s_c.arrive()
    each = z.own // z.f_groups
    for r in range(rd):
        block = slice(r * z.own, r * z.own + z.own)
        packed = jnp.concatenate([fbuf[n, r] for n in range(z.share)], axis=0).astype(F32)
        more = jnp.concatenate(
            [
                jnp.where(lane128 < z.f_more, pltpu.roll(packed[z.own :], (128 - g * z.f_more) % 128, 1), 0.0)
                for g in range(z.f_groups)
            ],
            axis=0,
        )
        eprime[block, 0:128] = packed[: z.own].astype(BF16)
        eprime[block, 128:256] = eprime[block, 128:256] + more.astype(BF16)
    gram_high, gram_low = split(mm(eprime[...], eprime[...], 0, 0))

    s_2.arrive()
    rows_all = planes * tokens
    picture = jnp.concatenate(
        [
            sum(pics[pi * z.tp + t].astype(F32) for t in range(z.tp)).astype(BF16)
            for pi in range(planes)
        ],
        axis=0,
    )
    halves = [mm(picture, cell[:, h * k : h * k + k]) for h in range(2)]
    l_hot.wait()
    hot = hot_ref[...].astype(F32)
    pieces = []
    for pi in range(planes):
        for h in range(2):
            pieces.append(
                halves[h][pi * half_rows : pi * half_rows + half_rows]
                + hot[h * half_rows : h * half_rows + half_rows]
            )
    cells = jnp.concatenate(pieces, axis=0)
    aug = (cells + mm(cells.astype(BF16), dm, 1, 1)).astype(BF16)
    aaug[...] = aug
    am[...] = mm(aug, gram_high) + mm(aug, gram_low)
    spread_in = jnp.sum(am[...] * aug.astype(F32), axis=1, keepdims=True) * (1.0 / z.width)
    inv_in = lax.rsqrt(jnp.maximum(spread_in, 0.0) + EPS_LAYER)
    invs[...] = jnp.broadcast_to(inv_in, (rows_all, 128))
    qkv[...] = (mm(aug, yh[...]) * inv_in).astype(BF16)

    unit = heads * tokens
    factor = 1.0 / math.sqrt(HEAD_DIM)
    row_u = lax.broadcasted_iota(jnp.int32, (unit, unit), 0)
    col_u = lax.broadcasted_iota(jnp.int32, (unit, unit), 1)
    same = row_u < 0
    for head in range(heads):
        low, high = head * tokens, head * tokens + tokens
        same = same | ((row_u >= low) & (row_u < high) & (col_u >= low) & (col_u < high))
    lane_u = lax.broadcasted_iota(jnp.int32, (1, unit), 1)

    def stacked(ref, pi, which):
        parts = [
            ref[pi * tokens : pi * tokens + tokens, (which * heads + h) * 128 : (which * heads + h) * 128 + 128]
            for h in range(heads)
        ]
        return jnp.concatenate(parts, axis=0) if heads > 1 else parts[0]

    for pi in range(planes):
        scores = mm(stacked(qkv, pi, 0), stacked(qkv, pi, 1), 1, 1) * factor
        if heads > 1:
            scores = jnp.where(same, scores, -1e30)
        top = jnp.max(scores, axis=1, keepdims=True)
        grown = jnp.exp(scores - top)
        soft = grown / jnp.sum(grown, axis=1, keepdims=True)
        prob[pi] = soft
        col_mean = jnp.sum(soft.astype(BF16).astype(F32), axis=0, keepdims=True) * (1.0 / tokens)
        per_head = jnp.concatenate(
            [
                jnp.where((lane_u >= h * tokens) & (lane_u < h * tokens + tokens), col_mean, 0.0)
                for h in range(heads)
            ]
            + [jnp.zeros((8 - heads, unit), F32)],
            axis=0,
        )
        high, low = split(per_head)
        value = stacked(qkv, pi, 2)
        result = mm(high, value) + mm(low, value)
        for h in range(heads):
            att[pi : pi + 1, h * 128 : h * 128 + 128] = result[h : h + 1]
    s_o.arrive()
    each = z.own // z.o_groups
    for r in range(rd):
        block = slice(r * z.own, r * z.own + z.own)
        main = obuf[r, 0 : z.own, :].astype(F32)
        for head in range(heads):
            low = head * HEAD_DIM
            first = max(min(HEAD_DIM, 128 - low), 0)
            moved = main if low == 0 else pltpu.roll(main, 128 - low, 1)
            moved = jnp.where(lane128 < first, moved, 0.0)
            if first < HEAD_DIM:
                extra = obuf[r, z.own :, :].astype(F32)
                moved = moved + jnp.concatenate(
                    [
                        jnp.where(
                            (lane128 >= first) & (lane128 < HEAD_DIM),
                            pltpu.roll(extra, (first - (low + first - 128) - g * z.o_more) % 128, 1),
                            0.0,
                        )
                        for g in range(z.o_groups)
                    ],
                    axis=0,
                )
            owin[block, head * 128 : head * 128 + 128] = moved.astype(BF16)
    if z.prow > planes:
        att[planes:, :] = jnp.zeros((z.prow - planes, heads * 128), F32)
    high, low = split(att[...])
    both = mm(jnp.concatenate([high, low], axis=0), owin[...], 1, 1)
    both = both[: z.prow] + both[z.prow :]
    part_width = z.width // z.mfold
    both = jnp.concatenate(
        [both[: 8 // z.mfold, f * part_width : f * part_width + part_width] for f in range(z.mfold)], axis=0
    )
    blocks = [both[:, block * 128 : block * 128 + 128] for block in range(part_width // 128)]
    blocks += [jnp.zeros((8, 128), F32)] * (len(blocks) % 2)
    mx_own[...] = jnp.concatenate(blocks, axis=0).astype(BF16)
    for offset in range(1, z.layer):
        index, where = neighbour(offset)
        s_mix.start(mx_own, mx.at[lay], where)
    mx[lay] = mx_own[...]
    means = [
        jnp.mean(aaug[pi * tokens : pi * tokens + tokens, :].astype(F32), axis=0, keepdims=True)
        for pi in range(planes)
    ]
    if z.prow > planes:
        means.append(jnp.zeros((z.prow - planes, k), F32))
    high, low = split(jnp.concatenate(means, axis=0))
    both = mm(jnp.concatenate([high, low], axis=0), eprime[...], 1, 1)
    pooled = both[: z.prow] + both[z.prow :]

    s_mix.arrive()
    mixed = mx[0].astype(F32)
    for index in range(1, z.layer):
        mixed = mixed + mx[index].astype(F32)
    mixed = jnp.concatenate(
        [mixed[block * 8 : block * 8 + 8] for block in range(z.width // z.mfold // 128)], axis=1
    )
    if z.mfold > 1:
        mixed = jnp.concatenate([mixed[f * planes : f * planes + planes] for f in range(z.mfold)], axis=1)
        mixed = jnp.concatenate([mixed, jnp.zeros((z.prow - planes, z.width), F32)], axis=0)
    pooled = pooled + mixed
    l_fin.wait()
    l_head.wait()
    final_gain, head_w = row(fin_ref), row(head_ref)
    centred = pooled - jnp.mean(pooled, axis=1, keepdims=True)
    inv_z = lax.rsqrt(jnp.mean(centred * centred, axis=1, keepdims=True) + EPS_LAYER)
    hat_z = centred * inv_z
    rewards = jnp.sum(hat_z * final_gain * head_w, axis=1, keepdims=True)
    mine = lax.broadcasted_iota(jnp.int32, (z.prow, 1), 0) == plane
    reward_ref[...] = jnp.sum(jnp.where(mine, rewards, 0.0), axis=0, keepdims=True)
    query = head_w * final_gain
    upstream = inv_z * (
        query - jnp.mean(query, axis=1, keepdims=True) - hat_z * jnp.mean(query * hat_z, axis=1, keepdims=True)
    )
    up16 = upstream.astype(BF16)
    share[...] = mm(up16, owin[...])
    uk[...] = mm(up16, eprime[...]) * (lay == 0).astype(F32)

    for pi in range(planes):
        q, key, value = (stacked(qkv, pi, which) for which in range(3))
        soft = prob[pi]
        parts = [
            jnp.broadcast_to(share[pi : pi + 1, h * 128 : h * 128 + 128], (tokens, 128)) for h in range(heads)
        ]
        given = (jnp.concatenate(parts, axis=0) if heads > 1 else parts[0]).astype(BF16)
        dprob = mm(given, value, 1, 1)
        dscores = (soft * (dprob - jnp.sum(dprob * soft, axis=1, keepdims=True)) * factor).astype(BF16)
        grads = [mm(dscores, key), mm(dscores, q, 0, 0), mm(soft.astype(BF16), given, 0, 0)]
        for which in range(3):
            for h in range(heads):
                dqkv[
                    pi * tokens : pi * tokens + tokens,
                    (which * heads + h) * 128 : (which * heads + h) * 128 + 128,
                ] = grads[which][h * tokens : h * tokens + tokens].astype(BF16)
    back = dqkv[...]
    inv_in = invs[:, 0:1]
    mean_two = jnp.sum(back.astype(F32) * qkv[...].astype(F32), axis=1, keepdims=True) * (1.0 / z.width)
    zk = inv_in * (mm(back, yh[...], 1, 1) - (mean_two * inv_in) * am[...])
    zk = zk + jnp.concatenate(
        [jnp.broadcast_to(uk[pi : pi + 1, :], (tokens, k)) for pi in range(planes)], axis=0
    )
    dcells = (zk + mm(zk.astype(BF16), dm)).astype(BF16)
    dpic = None
    for h in range(2):
        rows = jnp.concatenate(
            [dcells[pi * tokens + h * half_rows : pi * tokens + h * half_rows + half_rows] for pi in range(planes)],
            axis=0,
        )
        term = mm(rows, cell[:, h * k : h * k + k], 1, 1)
        dpic = term if dpic is None else dpic + term
    for pi in range(planes):
        dpart[pi] = dpic[pi * half_rows : pi * half_rows + half_rows].astype(BF16)
    for offset in range(1, z.layer):
        index, where = neighbour(offset)
        s_b2.start(dpart.at[index // z.tp], dbuf.at[lay], where)
    dbuf[lay] = dpart[plane]
    s_b2.arrive()
    total = dbuf[0].astype(F32)
    for index in range(1, z.layer):
        total = total + dbuf[index].astype(F32)
    total = total.astype(BF16).astype(F32)
    for r in range(rd):
        parts = [total[r * 8 : r * 8 + 8, b * 128 : b * 128 + 128] for b in range(3)]
        if r > 0:
            above = total[r * 8 - 8 : r * 8, 256:384]
            parts[0] = parts[0] + jnp.where(masks[0], pltpu.roll(above, 86, 1), 0.0)
        if r < rd - 1:
            below = total[r * 8 + 8 : r * 8 + 16, 0:128]
            parts[2] = parts[2] + jnp.where(masks[2], pltpu.roll(below, 42, 1), 0.0)
        sb2[r] = jnp.concatenate(parts, axis=1)
    for offset in range(1, rd):
        index, where = column(offset)
        s_b1.start(sb2.at[index], b1.at[me], where)
    b1[me] = sb2[me]
    s_b1.arrive()

    image_rows = slab * 8
    grads = jnp.concatenate([b1[slot_ref[0, j]] for j in range(slab)], axis=0)
    lane_s = lax.broadcasted_iota(jnp.int32, (image_rows, 128), 1)
    chunk_s = lax.rem(lax.broadcasted_iota(jnp.int32, (image_rows, 128), 0), 8)
    column_s = lax.rem(lane_s, CHUNK)
    from_left = (column_s == CHUNK - 1) & (chunk_s > 0)
    from_right = (column_s == 0) & (chunk_s < CHUNKS - 1)
    lines = []
    for y in range(ROWS):
        main = jnp.zeros((image_rows, 128), F32)
        for ky in range(3):
            block, j = divmod(y + 2 - ky, 3)
            shift = 42 * (ky - j) % 128
            moved = grads[:, block * 128 : block * 128 + 128]
            moved = moved if shift == 0 else pltpu.roll(moved, shift, 1)
            main = main + jnp.where((lane_s >= 42 * ky) & (lane_s < 42 * ky + 42), moved, 0.0)
        rim = jnp.where(from_left, pltpu.roll(main, 1, 0), 0.0)
        rim = jnp.where(from_right, pltpu.roll(main, image_rows - 1, 0), rim)
        lines.append(jnp.concatenate([main, rim], axis=1).astype(BF16))
    lines.append(jnp.zeros((image_rows, 256), BF16))
    lhs = jnp.concatenate(lines, axis=0)
    spread = mm(lhs, bandb[...])
    for block in range(CHUNK_BLOCKS):
        dact[block] = spread[:, block * 128 : block * 128 + 128]

    def gate(c, carry):
        at = pl.ds(pl.multiple_of(c * wide, 128), wide)
        parts = [
            dact[block, pl.ds(c, z.slab8, stride=8), :] for block in range(CHUNK_BLOCKS)
        ]
        gated = jnp.concatenate(parts, axis=1) * slope[:, at]
        slope[:, at] = gated
        return carry[0] + lanes_sum(gated), carry[1] + lanes_sum(gated * xs[:, at])

    first, second = lax.fori_loop(0, CHUNKS, gate, (zero, zero))
    bs_own[...] = total_rows(first, second)
    for offset in range(1, rd):
        index, where = column(offset)
        s_bst.start(bs_own, bs_buf.at[me], where)
    bs_buf[me] = bs_own[...]
    s_bst.arrive()
    both = group_means(bs_buf)
    one_t = jnp.concatenate([both[:slab]] * 8, axis=0)
    two_t = jnp.concatenate([both[slab:]] * 8, axis=0)

    def finish(c, carry):
        at = pl.ds(pl.multiple_of(c * wide, 128), wide)
        one = jnp.concatenate([one_t] * CHUNK_BLOCKS, axis=1)
        two = jnp.concatenate([two_t] * CHUNK_BLOCKS, axis=1)
        inv = jnp.concatenate([inverse_t] * CHUNK_BLOCKS, axis=1)
        value = inv * (slope[:, at] - one - xs[:, at] * two)
        for y in range(ROWS):
            grad_ref[y, :, at] = value[y * slab : y * slab + slab].astype(BF16)
        return carry

    lax.fori_loop(0, CHUNKS, finish, 0)
    for sender in sems:
        sender.finish()


def body(features, gn_gain, conv_w, patch_w, pos_emb, ln1_gain, qkv_w, out_w, final_gain, head_w, owner_slot):
    slab = features.shape[0]
    rd = lax.axis_size("rows")
    tp = lax.axis_size("tp")
    half_width = qkv_w.shape[2]
    heads_half = half_width // HEAD_DIM
    split_axes = ("grp", "img")
    if heads_half % (lax.axis_size("grp") * lax.axis_size("img")):
        split_axes = ("img",)
    split_sizes = tuple(lax.axis_size(axis) for axis in split_axes)
    planes = math.prod(split_sizes)
    heads = heads_half // planes
    z = Sizes(slab, rd, planes, tp, pos_emb.shape[1], heads * HEAD_DIM, heads, half_width)
    flat = features.shape[3]
    vmem = pl.BlockSpec(memory_space=pltpu.VMEM)
    anys = pl.BlockSpec(memory_space=pl.ANY)
    smem = pl.BlockSpec(memory_space=pltpu.SMEM)
    args = [
        (jnp.transpose(features.reshape(slab, ROWS, flat), (1, 0, 2)), anys),
        (gn_gain.reshape(1, -1), anys),
        (conv_w, anys),
        (patch_w, anys),
        (pos_emb, anys),
        (ln1_gain.reshape(-1, 128), anys),
        (jnp.transpose(qkv_w, (1, 0, 2)), anys),
        (out_w, anys),
        (final_gain.reshape(-1, 128), anys),
        (head_w.reshape(-1, 128), anys),
        (owner_slot, smem),
    ]
    spaces = [anys] * 9
    args += list(zip(tables(z), spaces))
    k, own, width, lay, tok = z.k, z.own, z.width, z.layer, z.tokens
    rows_all, unit = planes * tok, heads * tok
    half_rows = rd * CHUNKS
    two = 2 * slab

    def v(shape, dtype=F32):
        return pltpu.VMEM(shape, dtype)

    scratch = [
        v((ROWS, slab, flat), BF16), v(patch_w.shape, BF16), v((3, own, 256), BF16), v((own, 256), BF16),
        v((3 * PATCH * PATCH, k), BF16), v((32, 18 * 128), BF16), v((256, 7 * 64), BF16), v((384, 2 * k), BF16),
        v((z.pack, 3 * heads * 128), BF16),
        v((1, 64)), v(conv_w.shape, BF16), v(pos_emb.shape, BF16), v((width // 128, 128)), v((width // 128, 128)), v((width // 128, 128)),
        v((tok, k), BF16), v((tok, k), BF16), v((128, 128)), v((two, 2 * z.slab8)),
        v((z.slab8, flat)), v((z.slab8, flat)), v((z.slab8, flat + 256), BF16), v((32, 128)),
        v((1152, 128), BF16), v((256, 896), BF16), v((CHUNKS * z.slab8, 128)),
        v((slab, 8, 384)), v((slab, 8, 384)), v((rd, 8, 384)), v((lay, half_rows, 384), BF16), v((half_rows, 384), BF16),
        v((two, 128)), v((rd, two, 128)), v((8, 128)), v((rd, 8, 128)),
        v((k, z.pack), BF16), v((2, rd) + z.chunk, BF16), v((k, z.pack), BF16), v((k, 3 * heads * 128), BF16),
        v((width, k), BF16), v((width, heads * 128), BF16), v((z.win, k + 128)), v((k, k)),
        v((z.f_rows, 128), BF16), v((z.share, rd, z.f_part, 128), BF16), v((z.o_rows, 128), BF16), v((rd, z.o_rows, 128), BF16),
        v((1, width)),
        v((rows_all, k), BF16), v((rows_all, k)), v((rows_all, 3 * heads * 128), BF16), v((planes, unit, unit)),
        v((z.prow, heads * 128)), v((z.mrows, 128), BF16), v((lay, z.mrows, 128), BF16), v((rows_all, 3 * heads * 128), BF16),
        v((planes, half_rows, 384), BF16), v((lay, half_rows, 384), BF16), v((rd, 8, 384)), v((rd, 8, 384)),
        v((7, z.slab8 * 8, 128)), v((two, 128)), v((rd, two, 128)),
        v((rows_all, 128)), v((z.prow, heads * 128)), v((z.prow, k)),
        pltpu.SemaphoreType.DMA((19,)),
    ]
    for copies in [rd - 1] * 7 + [lay - 1] * 3 + [rd - 1] * 2 + [max(planes - 1, 1)] + [rd - 1] * 2 + [max(tp - 1, 1)]:
        scratch += [pltpu.SemaphoreType.DMA((copies,))] * 2
    grad, reward = pl.pallas_call(
        functools.partial(kernel, z, split_axes, split_sizes),
        out_shape=[
            jax.ShapeDtypeStruct((ROWS, slab, flat), BF16),
            jax.ShapeDtypeStruct((1, 1), F32),
        ],
        in_specs=[spec for _, spec in args],
        out_specs=[vmem, vmem],
        scratch_shapes=scratch,
        compiler_params=pltpu.CompilerParams(
            collective_id=0, has_side_effects=True, vmem_limit_bytes=58 * 2**20
        ),
    )(*[value for value, _ in args])
    return jnp.transpose(grad, (1, 0, 2)).reshape(slab, ROWS, 1, flat), reward.reshape(1)


def solution(mesh):
    placed = (
        P(("grp", "img"), "rows", "tp", None),
        P("tp"),
        P(None, None, None, "tp"),
        P("rows", None),
        P(),
        P(),
        P("rows", None, "tp"),
        P("rows", "tp"),
        P(),
        P(),
        P(("grp", "img"), None),
    )
    return jax.shard_map(
        body,
        mesh=mesh,
        in_specs=placed,
        out_specs=(P(("grp", "img"), "rows", "tp", None), P(("grp", "img", "rows"))),
        check_vma=False,
    )
```

```python
import functools
import math

import jax
import jax.numpy as jnp
import numpy as np
from jax import lax
from jax.experimental import pallas as pl
from jax.experimental.pallas import tpu as pltpu
from jax.sharding import PartitionSpec as P

C = 128
GROUPS = 32
PATCH = 14
HEAD_DIM = 80
W = 112
CHUNK = 14
CHUNKS = W // CHUNK
ROWS = 7
CELL = 152
CELL_USED = 147
EPS_GROUP = 1e-06
EPS_LAYER = 1e-05
F32 = jnp.float32
BF16 = jnp.bfloat16
EXACT = lax.Precision.HIGHEST


def up(count, step):
    return (count + step - 1) // step * step


def mm(left, right, left_dim=1, right_dim=0, precision=None):
    return lax.dot_general(
        left, right, (((left_dim,), (right_dim,)), ((), ())),
        preferred_element_type=F32, precision=precision,
    )


def split(values):
    high = values.astype(BF16)
    return high, (values - high.astype(F32)).astype(BF16)


class Sizes:
    def __init__(self, slab, rows_devices, planes, tp, width, span, heads, half_width):
        self.slab = slab
        self.rows_devices = rows_devices
        self.planes = planes
        self.tp = tp
        self.layer = planes * tp
        self.width = width
        self.span = span
        self.heads = heads
        self.half_width = half_width
        self.tokens = rows_devices * 2 * CHUNKS
        self.own = width // rows_devices
        self.ones = CELL + self.tokens
        self.k = up(up(self.ones + rows_devices, 32 * rows_devices), 256)
        self.pack = up(3 * span, 128)
        self.by_lanes = self.pack == 128 * rows_devices
        if self.by_lanes:
            self.chunk = (up(self.ones + rows_devices, 32) // 2, 128)
        else:
            self.chunk = (self.k // rows_devices // 2, self.pack)
        self.win = up(min(self.own + 127, width), 128)
        self.slab8 = 8 * slab
        self.prow = up(planes, 8)
        self.mfold = 8 // planes if planes <= 4 else 1
        self.mrows = up(width // self.mfold // 128 * 8, 16)
        self.f_more = CELL_USED - 128
        self.f_groups = 128 // self.f_more
        while self.own % (16 * self.f_groups):
            self.f_groups -= 1
        self.f_rows = self.own + self.own // self.f_groups
        self.share = self.layer if self.f_rows % (16 * self.layer) == 0 else tp
        self.f_part = self.f_rows // self.share
        self.o_more = max(span - 128, 0)
        self.o_groups = 128 // self.o_more if self.o_more else 1
        self.o_rows = self.own + (self.own // self.o_groups if self.o_more else 0)


def tables(z):
    fold = np.zeros((3 * PATCH * PATCH, z.k), np.float32)
    for entry in range(3 * PATCH * PATCH):
        pixel, colour = divmod(entry, 3)
        row, col = divmod(pixel, PATCH)
        fold[entry, colour * 49 + row // 2 * 7 + col // 2] = 1
    place_f = np.zeros((32, 18 * 128), np.float32)
    place_b = np.zeros((256, 7 * 64), np.float32)
    for colour in range(3):
        for ky in range(3):
            for kx in range(3):
                tap = colour * 9 + ky * 3 + kx
                for xx in range(CHUNK):
                    lane = 42 * ky + 14 * colour + xx
                    place_f[tap, (xx + kx + 1) * 128 + lane] = 1
                    out = xx + kx - 1
                    if 0 <= out < CHUNK:
                        place_b[lane, out // 2 * 64 + out % 2 * 32 + tap] = 1
                if kx == 2:
                    place_b[128 + 42 * ky + 14 * colour + 13, tap] = 1
                if kx == 0:
                    place_b[128 + 42 * ky + 14 * colour, 6 * 64 + 32 + tap] = 1
    cell = np.zeros((384, 2 * z.k), np.float32)
    for half in range(2):
        for row in range(ROWS):
            for colour in range(3):
                for col in range(7):
                    line = row + 1
                    cell[line // 3 * 128 + line % 3 * 42 + colour * 14 + half * 7 + col,
                         half * z.k + colour * 49 + row * 7 + col] = 1
    rd = z.rows_devices
    hot = np.zeros((z.tokens, z.k), np.float32)
    for half in range(2):
        for r in range(rd):
            for c in range(CHUNKS):
                hot[half * rd * CHUNKS + r * CHUNKS + c, CELL + r * 2 * CHUNKS + 2 * c + half] = 1
    selpos = np.zeros((z.tokens, z.k), np.float32)
    selpos[np.arange(z.tokens), CELL + np.arange(z.tokens)] = 1
    pick = np.zeros((z.pack, 3 * z.heads * 128), np.float32)
    for which in range(3):
        for head in range(z.heads):
            for lane in range(HEAD_DIM):
                pick[which * z.span + head * HEAD_DIM + lane, (which * z.heads + head) * 128 + lane] = 1
    group = np.zeros((128, 128), np.float32)
    lanes = np.arange(128)
    group[lanes[:, None] % 64 // 4 == lanes[None, :] % 64 // 4] = 1
    rowsel = np.zeros((2 * z.slab, 2 * z.slab8), np.float32)
    for s in range(z.slab):
        for y in range(ROWS):
            rowsel[s, y * z.slab + s] = 1
            rowsel[z.slab + s, z.slab8 + y * z.slab + s] = 1
    bf = lambda a: jnp.asarray(a, BF16)
    return [bf(fold), bf(place_f), bf(place_b), bf(cell), bf(hot), bf(selpos), bf(pick),
            jnp.asarray(group, F32), jnp.asarray(rowsel, F32)]


class Sender:
    def __init__(self, sems):
        self.send, self.recv = sems
        self.copies = []

    def start(self, src, dst, where):
        at = len(self.copies)
        copy = pltpu.make_async_remote_copy(
            src_ref=src, dst_ref=dst, send_sem=self.send.at[at], recv_sem=self.recv.at[at],
            device_id=where, device_id_type=pl.DeviceIdType.MESH,
        )
        copy.start()
        self.copies.append(copy)

    def arrive(self):
        for copy in self.copies:
            copy.wait_recv()

    def finish(self):
        for copy in self.copies:
            copy.wait_send()


def kernel(
    z, split_axes, split_sizes,
    feat_hbm, gn_hbm, conv_hbm, patch_hbm, pos_hbm, ln1_hbm, qkv_hbm, out_hbm, fin_hbm, head_hbm, slot_ref,
    fold_hbm, placef_hbm, placeb_hbm, cell_hbm, hot_hbm, selpos_hbm, pick_hbm, group_hbm, rowsel_hbm,
    grad_ref, reward_ref,
    feat, patch, qkvw, outw, fold, placef, placeb, cell, pick,
    gn_ref, conv_ref, pos_ref, ln1_ref, fin_ref, head_ref, hot_ref, selpos_ref, group_ref, rowsel_ref,
    xs, slope, act, cwf, bandf, bandb, tmp_t, out1, sb1, p1, pics, pp,
    stat_own, stat_buf, mean_own, mean_buf, ypart, rsbuf, yfull, yh, eprime, owin, posw, dmat,
    fpack, fbuf, opack, obuf, ln1_row,
    aaug, am, qkv, prob, att, mx_own, mx, dqkv, dpart, dbuf, sb2, b1, dact, bs_own, bs_buf,
    invs, share, uk,
    local_sems, *remote,
):
    sems = [Sender(remote[2 * i : 2 * i + 2]) for i in range(len(remote) // 2)]
    s_stat, s_mean, s_rs, s_ag, s_e, s_o, s_1, s_2, s_mix, s_b2, s_b1, s_bst, s_f, s_rs2, s_ag2, s_c = sems
    rd, slab, tokens, k = z.rows_devices, z.slab, z.tokens, z.k
    planes, heads, span = z.planes, z.heads, z.span
    me = lax.axis_index("rows")
    plane = 0
    for axis, size in zip(split_axes, split_sizes):
        plane = plane * size + lax.axis_index(axis)
    tp = lax.axis_index("tp")
    lay = plane * z.tp + tp

    def column(offset):
        index = lax.rem(me + offset, rd)
        return index, {"rows": index}

    def place(rest, where):
        for axis, size in reversed(list(zip(split_axes, split_sizes))):
            where[axis] = lax.rem(rest, size)
            rest = rest // size
        return where

    def neighbour(offset):
        index = lax.rem(lay + offset, z.layer)
        return index, place(index // z.tp, {"tp": lax.rem(index, z.tp)})

    def fellow(offset):
        index = lax.rem(plane + offset, planes)
        return index, place(index, {})

    def row(ref):
        return jnp.concatenate([ref[i : i + 1, :] for i in range(ref.shape[0])], axis=1)

    start = jnp.minimum(plane * span // 128 * 128, z.half_width - 256)
    start = pl.multiple_of(start, 128)
    inside = plane * span - start
    window = pl.ds(start, 256)
    loads = []

    def load(src, dst):
        copy = pltpu.make_async_copy(src, dst, local_sems.at[len(loads)])
        copy.start()
        loads.append(copy)
        return copy

    l_feat = load(feat_hbm, feat)
    l_out = load(out_hbm.at[:, window], outw)
    l_rowsel = load(rowsel_hbm, rowsel_ref)

    barrier = pltpu.get_barrier_semaphore()
    for offset in range(1, rd):
        pl.semaphore_signal(barrier, inc=1, device_id=column(offset)[1], device_id_type=pl.DeviceIdType.MESH)
    for offset in range(1, z.layer):
        pl.semaphore_signal(barrier, inc=1, device_id=neighbour(offset)[1], device_id_type=pl.DeviceIdType.MESH)

    l_pos = load(pos_hbm, pos_ref)
    l_selpos = load(selpos_hbm, selpos_ref)
    l_ln1 = load(ln1_hbm, ln1_ref)
    l_patch = load(patch_hbm, patch)
    l_fold = load(fold_hbm, fold)
    l_qkv = load(qkv_hbm.at[:, :, window], qkvw)
    l_conv = load(conv_hbm, conv_ref)
    l_pf = load(placef_hbm, placef)
    l_pb = load(placeb_hbm, placeb)
    l_group = load(group_hbm, group_ref)
    l_gn = load(gn_hbm, gn_ref)
    l_pick = load(pick_hbm, pick)
    l_cell = load(cell_hbm, cell)
    l_hot = load(hot_hbm, hot_ref)
    l_fin = load(fin_hbm, fin_ref)
    l_head = load(head_hbm, head_ref)

    flat = CHUNKS * CHUNK * 64
    wide = CHUNK * 64
    used = ROWS * slab
    count = rd * ROWS * W * (C // GROUPS)

    def total_rows(first, second):
        return mm(rowsel_ref[...], jnp.concatenate([first, second], axis=0), precision=EXACT)

    def lanes_sum(values):
        total = values[:, 0:128]
        for block in range(1, values.shape[1] // 128):
            total = total + values[:, block * 128 : block * 128 + 128]
        return total

    lane128 = lax.broadcasted_iota(jnp.int32, (1, 128), 1)

    def pack_out():
        l_out.wait()
        ow = pltpu.roll(outw[...].astype(F32), lax.rem(256 - inside, 256), 1)
        opack[0 : z.own, :] = ow[:, :128].astype(BF16)
        if z.o_more:
            each = z.own // z.o_groups
            more = jnp.where(lane128 < z.o_more, ow[:, 128:], 0.0)
            packed = more[:each]
            for g in range(1, z.o_groups):
                packed = packed + pltpu.roll(more[g * each : g * each + each], g * z.o_more, 1)
            opack[z.own :, :] = packed.astype(BF16)

    ahead = z.o_rows * 9 // 32 // 16 * 16
    early = pl.ds(0, ahead)
    late = pl.ds(ahead, z.o_rows - ahead)
    pack_out()
    pl.semaphore_wait(barrier, rd - 1 + z.layer - 1)
    for offset in range(1, rd):
        index, where = column(offset)
        s_o.start(opack.at[early], obuf.at[me, early], where)

    l_feat.wait()
    xs[used:, :] = jnp.zeros((z.slab8 - used, flat), F32)
    for y in range(ROWS):
        xs[y * slab : y * slab + slab, :] = feat[y].astype(F32)

    def stats(c, carry):
        x = xs[:, pl.ds(pl.multiple_of(c * wide, 128), wide)]
        return carry[0] + lanes_sum(x), carry[1] + lanes_sum(x * x)

    zero = jnp.zeros((z.slab8, 128), F32)
    first, second = lax.fori_loop(0, CHUNKS, stats, (zero, zero))
    l_rowsel.wait()
    stat_own[...] = total_rows(first, second)
    for offset in range(1, rd):
        index, where = column(offset)
        s_stat.start(stat_own, stat_buf.at[me], where)
    stat_buf[me] = stat_own[...]

    begin = me * z.own
    l_pos.wait()
    l_selpos.wait()
    l_ln1.wait()
    wstart = jnp.minimum(begin // 128 * 128, z.width - z.win)
    wstart = pl.multiple_of(wstart, 128)
    wlanes = pl.ds(wstart, z.win)
    posw[:, :k] = mm(pos_ref[:, wlanes], selpos_ref[...], 0, 0)
    ln1_row[...] = row(ln1_ref)
    gains = jnp.broadcast_to(ln1_row[:, wlanes], (8, z.win)) * 0.125
    posw[:, k:] = mm(gains, jnp.ones((8, 128), F32), 0, 0, EXACT)
    own_rows = pl.ds(pl.multiple_of(begin - wstart, 16), z.own)
    l_patch.wait()
    l_fold.wait()
    e_own = mm(patch[...], fold[...]) + posw[own_rows, :k]
    mean = jnp.mean(e_own, axis=0, keepdims=True)
    mean_own[...] = jnp.zeros((8, 128), F32)
    for block in range(k // 128):
        mean_own[block : block + 1, :] = mean[:, block * 128 : block * 128 + 128]
    lane_k = lax.broadcasted_iota(jnp.int32, (1, k), 1)
    lane128 = lax.broadcasted_iota(jnp.int32, (1, 128), 1)
    e_own = e_own - mean + (lane_k == z.ones + me).astype(F32)
    gcol = posw[own_rows, k:]
    fpack[0 : z.own, :] = e_own[:, :128].astype(BF16)
    more = jnp.where(lane128 < z.f_more, e_own[:, 128:256], 0.0)
    each = z.own // z.f_groups
    packed = more[:each]
    for g in range(1, z.f_groups):
        packed = packed + pltpu.roll(more[g * each : g * each + each], g * z.f_more, 1)
    fpack[z.own :, :] = packed.astype(BF16)
    e_gain = (e_own * jnp.concatenate([gcol] * (k // 128), axis=1)).astype(BF16)
    l_qkv.wait()
    blocks = [jnp.zeros((k, 128), F32) for _ in range(z.pack // 128)]
    lane256 = lax.broadcasted_iota(jnp.int32, (1, 256), 1)
    for which in range(3):
        part = mm(e_gain, qkvw[which], 0, 0)
        base, off = divmod(span * which, 128)
        part = pltpu.roll(part, lax.rem(off - inside + 512, 256), 1)
        part = jnp.where((lane256 >= off) & (lane256 < off + span), part, 0.0)
        blocks[base] = blocks[base] + part[:, :128]
        if off + span > 128:
            blocks[base + 1] = blocks[base + 1] + part[:, 128:]
    ypart[...] = jnp.concatenate(blocks, axis=1).astype(BF16)

    def part_of(index, half):
        tall = z.chunk[0]
        if z.by_lanes:
            return pl.ds(half * tall, tall), pl.ds(pl.multiple_of(index * 128, 128), 128)
        return pl.ds(pl.multiple_of((2 * index + half) * tall, 16), tall), slice(None)

    share_me = tp * planes + plane if z.share == z.layer else tp
    f_mine = pl.ds(pl.multiple_of(share_me * z.f_part, 16), z.f_part)
    for offset in range(1, rd):
        index, where = column(offset)
        s_e.start(fpack.at[f_mine], fbuf.at[share_me, me], where)
    fbuf[share_me, me] = fpack[f_mine, :]
    for half, sender in enumerate((s_rs, s_rs2)):
        for offset in range(1, rd):
            index, where = column(offset)
            sender.start(ypart.at[part_of(index, half)], rsbuf.at[half, me], where)
        rsbuf[half, me] = ypart[part_of(me, half)]
    for offset in range(1, rd):
        index, where = column(offset)
        s_mean.start(mean_own, mean_buf.at[me], where)
    mean_buf[me] = mean_own[...]
    l_conv.wait()
    cwf[...] = jnp.zeros((32, 128), F32)
    for colour in range(3):
        for ky in range(3):
            cwf[pl.ds(9 * colour + 3 * ky, 3), 0:64] = conv_ref[colour, ky].astype(F32)
    taps = cwf[...]
    l_pf.wait()
    spread = mm(taps[:, :64].astype(BF16), placef[...], 0, 0).astype(BF16)
    for px in range(18):
        bandf[px * 64 : px * 64 + 64, :] = spread[:, px * 128 : px * 128 + 128]
    act[:, 0:128] = jnp.zeros((z.slab8, 128), BF16)
    act[:, 128 + flat :] = jnp.zeros((z.slab8, 128), BF16)

    l_group.wait()
    l_gn.wait()
    s_stat.arrive()

    def tile(per_image):
        return jnp.concatenate([jnp.concatenate([per_image] * 8, axis=0)] * CHUNK_BLOCKS, axis=1)

    CHUNK_BLOCKS = wide // 128
    gain = jnp.concatenate([gn_ref[...], gn_ref[...]], axis=1)
    gain_wide = jnp.concatenate([gain] * CHUNK_BLOCKS, axis=1)

    def group_means(buf):
        total = buf[0]
        for r in range(1, rd):
            total = total + buf[r]
        return mm(total, group_ref[...], precision=EXACT) * (1.0 / count)

    both = group_means(stat_buf)
    average = both[:slab]
    inverse = lax.rsqrt(both[slab:] - average * average + EPS_GROUP)
    average_t = jnp.concatenate([average] * 8, axis=0)
    inverse_t = jnp.concatenate([inverse] * 8, axis=0)

    def activate(c, carry):
        at = pl.ds(pl.multiple_of(c * wide, 128), wide)
        x = xs[:, at]
        avg = jnp.concatenate([average_t] * CHUNK_BLOCKS, axis=1)
        inv = jnp.concatenate([inverse_t] * CHUNK_BLOCKS, axis=1)
        normed = (x - avg) * inv
        scaled = normed * gain_wide
        sig = 0.5 * jnp.tanh(0.5 * scaled) + 0.5
        xs[:, at] = normed
        active = scaled * sig
        act[:, pl.ds(pl.multiple_of(c * wide + 128, 128), wide)] = active.astype(BF16)
        slope[:, at] = sig * (1.0 + scaled - active) * gain_wide
        return carry

    lax.fori_loop(0, CHUNKS, activate, 0)
    lhs = jnp.concatenate([act[:, wide * c : wide * c + wide + 256] for c in range(CHUNKS)], axis=0)
    tmp_t[...] = mm(lhs, bandf[...])
    lane = lax.broadcasted_iota(jnp.int32, (8, 128), 1)

    def slot_mask(slot):
        return (lane >= 42 * slot) & (lane < 42 * slot + 42)

    masks = [slot_mask(j) for j in range(3)]

    def message(s, carry):
        acc = [jnp.zeros((8, 128), F32) for _ in range(3)]
        for y in range(ROWS):
            value = tmp_t[pl.ds(y * slab + s, 8, stride=z.slab8), :]
            for ky in range(3):
                block, j = divmod(y - ky + 2, 3)
                shift = 42 * (j - ky) % 128
                moved = value if shift == 0 else pltpu.roll(value, shift, 1)
                acc[block] = acc[block] + jnp.where(masks[j], moved, 0.0)
        out1[s] = jnp.concatenate(acc, axis=1)
        return carry

    for s in range(slab):
        message(s, 0)
    for slot in range(slab):
        source = 0
        for j in range(slab):
            source = jnp.where(slot_ref[0, j] == slot, j, source)
        sb1[slot] = out1[source]
    for offset in range(1, rd):
        index, where = column(offset)
        s_1.start(sb1.at[index], p1.at[me], where)
    p1[me] = sb1[me]

    def taps_back():
        l_pb.wait()
        tap64 = taps[:, :64]
        none = jnp.zeros((32, 64), F32)
        double = jnp.concatenate(
            [jnp.concatenate([tap64, none], axis=1), jnp.concatenate([none, tap64], axis=1)], axis=0
        ).astype(BF16)
        for pair in range(7):
            bandb[:, pair * 128 : pair * 128 + 128] = mm(
                placeb[:, pair * 64 : pair * 64 + 64], double
            ).astype(BF16)
        for r in range(rd):
            block = slice(r * z.own, r * z.own + z.own)
            pos = mm(pos_ref[:, block], selpos_ref[...], 0, 0)
            pos = pos - jnp.mean(pos, axis=0, keepdims=True) + (lane_k == z.ones + r).astype(F32)
            eprime[block, 128:] = pos[:, 128:].astype(BF16)

    if z.by_lanes and 2 * z.chunk[0] < k:
        yfull[2 * z.chunk[0] :, :] = jnp.zeros((k - 2 * z.chunk[0], z.pack), BF16)
    s_e.arrive()
    if z.share == z.layer:
        for offset in range(1, planes):
            index, where = fellow(offset)
            s_f.start(fbuf.at[share_me], fbuf.at[share_me], where)
    for half, (sender, after) in enumerate(((s_rs, s_ag), (s_rs2, s_ag2))):
        sender.arrive()
        total = rsbuf[half, 0].astype(F32)
        for r in range(1, rd):
            total = total + rsbuf[half, r].astype(F32)
        yfull[part_of(me, half)] = total.astype(BF16)
        for offset in range(1, rd):
            index, where = column(offset)
            after.start(yfull.at[part_of(me, half)], yfull.at[part_of(me, half)], where)
        if half == 0:
            taps_back()
    for offset in range(1, rd):
        index, where = column(offset)
        s_o.start(opack.at[late], obuf.at[me, late], where)
    obuf[me] = opack[...]
    s_1.arrive()
    slabs = [p1[r] for r in range(rd)]
    keep = [lane >= 42, lane >= 0, lane < 84]
    for r in range(rd):
        parts = [jnp.where(keep[b], slabs[r][:, b * 128 : b * 128 + 128], 0.0) for b in range(3)]
        parts[1] = jnp.where(lane < 126, parts[1], 0.0)
        parts[0] = jnp.where(lane < 126, parts[0], 0.0)
        if r > 0:
            parts[0] = parts[0] + jnp.where(masks[1], pltpu.roll(slabs[r - 1][:, 256:384], 86, 1), 0.0)
        if r < rd - 1:
            parts[2] = parts[2] + jnp.where(masks[1], pltpu.roll(slabs[r + 1][:, 0:128], 42, 1), 0.0)
        tmp_t[pl.ds(r * 8, 8), :] = parts[0]
        tmp_t[pl.ds(rd * 8 + r * 8, 8), :] = parts[1]
        tmp_t[pl.ds(2 * rd * 8 + r * 8, 8), :] = parts[2]
    half_rows = rd * CHUNKS
    pp[...] = jnp.concatenate(
        [tmp_t[b * half_rows : b * half_rows + half_rows, :] for b in range(3)], axis=1
    ).astype(BF16)
    for offset in range(1, z.layer):
        index, where = neighbour(offset)
        s_2.start(pp, pics.at[lay], where)
    pics[lay] = pp[...]

    s_f.arrive()
    group_size = z.share // z.tp
    group = fbuf.at[pl.ds(tp * group_size, group_size)]
    for offset in range(1, z.tp):
        s_c.start(group, group, {"tp": lax.rem(tp + offset, z.tp)})
    s_mean.arrive()
    dmat[...] = jnp.zeros((k, k), F32)
    block_means = [
        jnp.concatenate([mean_buf[r, block : block + 1, :] for block in range(k // 128)], axis=1) for r in range(rd)
    ]
    middle = sum(block_means) * (1.0 / rd)
    for r in range(rd):
        dmat[z.ones + r : z.ones + r + 1, :] = block_means[r] - middle
    dm = dmat[...].astype(BF16)
    l_pick.wait()
    l_cell.wait()
    s_ag.arrive()
    s_ag2.arrive()
    yh[...] = mm(yfull[...], pick[...]).astype(BF16)
    s_c.arrive()
    each = z.own // z.f_groups
    for r in range(rd):
        block = slice(r * z.own, r * z.own + z.own)
        packed = jnp.concatenate([fbuf[n, r] for n in range(z.share)], axis=0).astype(F32)
        more = jnp.concatenate(
            [
                jnp.where(lane128 < z.f_more, pltpu.roll(packed[z.own :], (128 - g * z.f_more) % 128, 1), 0.0)
                for g in range(z.f_groups)
            ],
            axis=0,
        )
        eprime[block, 0:128] = packed[: z.own].astype(BF16)
        eprime[block, 128:256] = eprime[block, 128:256] + more.astype(BF16)
    gram_high, gram_low = split(mm(eprime[...], eprime[...], 0, 0))

    s_2.arrive()
    rows_all = planes * tokens
    picture = jnp.concatenate(
        [
            sum(pics[pi * z.tp + t].astype(F32) for t in range(z.tp)).astype(BF16)
            for pi in range(planes)
        ],
        axis=0,
    )
    halves = [mm(picture, cell[:, h * k : h * k + k]) for h in range(2)]
    l_hot.wait()
    hot = hot_ref[...].astype(F32)
    pieces = []
    for pi in range(planes):
        for h in range(2):
            pieces.append(
                halves[h][pi * half_rows : pi * half_rows + half_rows]
                + hot[h * half_rows : h * half_rows + half_rows]
            )
    cells = jnp.concatenate(pieces, axis=0)
    aug = (cells + mm(cells.astype(BF16), dm, 1, 1)).astype(BF16)
    aaug[...] = aug
    am[...] = mm(aug, gram_high) + mm(aug, gram_low)
    spread_in = jnp.sum(am[...] * aug.astype(F32), axis=1, keepdims=True) * (1.0 / z.width)
    inv_in = lax.rsqrt(jnp.maximum(spread_in, 0.0) + EPS_LAYER)
    invs[...] = jnp.broadcast_to(inv_in, (rows_all, 128))
    qkv[...] = (mm(aug, yh[...]) * inv_in).astype(BF16)

    unit = heads * tokens
    factor = 1.0 / math.sqrt(HEAD_DIM)
    row_u = lax.broadcasted_iota(jnp.int32, (unit, unit), 0)
    col_u = lax.broadcasted_iota(jnp.int32, (unit, unit), 1)
    same = row_u < 0
    for head in range(heads):
        low, high = head * tokens, head * tokens + tokens
        same = same | ((row_u >= low) & (row_u < high) & (col_u >= low) & (col_u < high))
    lane_u = lax.broadcasted_iota(jnp.int32, (1, unit), 1)

    def stacked(ref, pi, which):
        parts = [
            ref[pi * tokens : pi * tokens + tokens, (which * heads + h) * 128 : (which * heads + h) * 128 + 128]
            for h in range(heads)
        ]
        return jnp.concatenate(parts, axis=0) if heads > 1 else parts[0]

    for pi in range(planes):
        scores = mm(stacked(qkv, pi, 0), stacked(qkv, pi, 1), 1, 1) * factor
        if heads > 1:
            scores = jnp.where(same, scores, -1e30)
        top = jnp.max(scores, axis=1, keepdims=True)
        grown = jnp.exp(scores - top)
        soft = grown * (1.0 / jnp.sum(grown, axis=1, keepdims=True))
        prob[pi] = soft
        col_mean = jnp.sum(soft.astype(BF16).astype(F32), axis=0, keepdims=True) * (1.0 / tokens)
        per_head = jnp.concatenate(
            [
                jnp.where((lane_u >= h * tokens) & (lane_u < h * tokens + tokens), col_mean, 0.0)
                for h in range(heads)
            ]
            + [jnp.zeros((8 - heads, unit), F32)],
            axis=0,
        )
        high, low = split(per_head)
        value = stacked(qkv, pi, 2)
        result = mm(high, value) + mm(low, value)
        for h in range(heads):
            att[pi : pi + 1, h * 128 : h * 128 + 128] = result[h : h + 1]
    each = z.own // z.o_groups
    for offset in range(rd):
        if offset:
            s_o.copies[offset - 1].wait_recv()
            s_o.copies[rd - 1 + offset - 1].wait_recv()
        r = lax.rem(me + rd - offset, rd)
        block = pl.ds(pl.multiple_of(r * z.own, 16), z.own)
        main = obuf[r, 0 : z.own, :].astype(F32)
        for head in range(heads):
            low = head * HEAD_DIM
            first = max(min(HEAD_DIM, 128 - low), 0)
            moved = main if low == 0 else pltpu.roll(main, 128 - low, 1)
            moved = jnp.where(lane128 < first, moved, 0.0)
            if first < HEAD_DIM:
                extra = obuf[r, z.own :, :].astype(F32)
                moved = moved + jnp.concatenate(
                    [
                        jnp.where(
                            (lane128 >= first) & (lane128 < HEAD_DIM),
                            pltpu.roll(extra, (first - (low + first - 128) - g * z.o_more) % 128, 1),
                            0.0,
                        )
                        for g in range(z.o_groups)
                    ],
                    axis=0,
                )
            owin[block, head * 128 : head * 128 + 128] = moved.astype(BF16)
    if z.prow > planes:
        att[planes:, :] = jnp.zeros((z.prow - planes, heads * 128), F32)
    high, low = split(att[...])
    both = mm(jnp.concatenate([high, low], axis=0), owin[...], 1, 1)
    both = both[: z.prow] + both[z.prow :]
    part_width = z.width // z.mfold
    both = jnp.concatenate(
        [both[: 8 // z.mfold, f * part_width : f * part_width + part_width] for f in range(z.mfold)], axis=0
    )
    blocks = [both[:, block * 128 : block * 128 + 128] for block in range(part_width // 128)]
    blocks += [jnp.zeros((8, 128), F32)] * (len(blocks) % 2)
    mx_own[...] = jnp.concatenate(blocks, axis=0).astype(BF16)
    for offset in range(1, z.layer):
        index, where = neighbour(offset)
        s_mix.start(mx_own, mx.at[lay], where)
    mx[lay] = mx_own[...]
    means = [
        jnp.mean(aaug[pi * tokens : pi * tokens + tokens, :].astype(F32), axis=0, keepdims=True)
        for pi in range(planes)
    ]
    if z.prow > planes:
        means.append(jnp.zeros((z.prow - planes, k), F32))
    high, low = split(jnp.concatenate(means, axis=0))
    both = mm(jnp.concatenate([high, low], axis=0), eprime[...], 1, 1)
    pooled = both[: z.prow] + both[z.prow :]

    s_mix.arrive()
    mixed = mx[0].astype(F32)
    for index in range(1, z.layer):
        mixed = mixed + mx[index].astype(F32)
    mixed = jnp.concatenate(
        [mixed[block * 8 : block * 8 + 8] for block in range(z.width // z.mfold // 128)], axis=1
    )
    if z.mfold > 1:
        mixed = jnp.concatenate([mixed[f * planes : f * planes + planes] for f in range(z.mfold)], axis=1)
        mixed = jnp.concatenate([mixed, jnp.zeros((z.prow - planes, z.width), F32)], axis=0)
    pooled = pooled + mixed
    l_fin.wait()
    l_head.wait()
    final_gain, head_w = row(fin_ref), row(head_ref)
    centred = pooled - jnp.mean(pooled, axis=1, keepdims=True)
    inv_z = lax.rsqrt(jnp.mean(centred * centred, axis=1, keepdims=True) + EPS_LAYER)
    hat_z = centred * inv_z
    rewards = jnp.sum(hat_z * final_gain * head_w, axis=1, keepdims=True)
    mine = lax.broadcasted_iota(jnp.int32, (z.prow, 1), 0) == plane
    reward_ref[...] = jnp.sum(jnp.where(mine, rewards, 0.0), axis=0, keepdims=True)
    query = head_w * final_gain
    upstream = inv_z * (
        query - jnp.mean(query, axis=1, keepdims=True) - hat_z * jnp.mean(query * hat_z, axis=1, keepdims=True)
    )
    up16 = upstream.astype(BF16)
    share[...] = mm(up16, owin[...])
    uk[...] = mm(up16, eprime[...]) * (lay == 0).astype(F32)

    for pi in range(planes):
        q, key, value = (stacked(qkv, pi, which) for which in range(3))
        soft = prob[pi]
        parts = [
            jnp.broadcast_to(share[pi : pi + 1, h * 128 : h * 128 + 128], (tokens, 128)) for h in range(heads)
        ]
        given = (jnp.concatenate(parts, axis=0) if heads > 1 else parts[0]).astype(BF16)
        dprob = mm(given, value, 1, 1)
        dscores = (soft * (dprob - jnp.sum(dprob * soft, axis=1, keepdims=True)) * factor).astype(BF16)
        grads = [mm(dscores, key), mm(dscores, q, 0, 0), mm(soft.astype(BF16), given, 0, 0)]
        for which in range(3):
            for h in range(heads):
                dqkv[
                    pi * tokens : pi * tokens + tokens,
                    (which * heads + h) * 128 : (which * heads + h) * 128 + 128,
                ] = grads[which][h * tokens : h * tokens + tokens].astype(BF16)
    back = dqkv[...]
    inv_in = invs[:, 0:1]
    mean_two = jnp.sum(back.astype(F32) * qkv[...].astype(F32), axis=1, keepdims=True) * (1.0 / z.width)
    zk = inv_in * (mm(back, yh[...], 1, 1) - (mean_two * inv_in) * am[...])
    zk = zk + jnp.concatenate(
        [jnp.broadcast_to(uk[pi : pi + 1, :], (tokens, k)) for pi in range(planes)], axis=0
    )
    dcells = (zk + mm(zk.astype(BF16), dm)).astype(BF16)
    dpic = None
    for h in range(2):
        rows = jnp.concatenate(
            [dcells[pi * tokens + h * half_rows : pi * tokens + h * half_rows + half_rows] for pi in range(planes)],
            axis=0,
        )
        term = mm(rows, cell[:, h * k : h * k + k], 1, 1)
        dpic = term if dpic is None else dpic + term
    for pi in range(planes):
        dpart[pi] = dpic[pi * half_rows : pi * half_rows + half_rows].astype(BF16)
    for offset in range(1, z.layer):
        index, where = neighbour(offset)
        s_b2.start(dpart.at[index // z.tp], dbuf.at[lay], where)
    dbuf[lay] = dpart[plane]
    s_b2.arrive()
    total = dbuf[0].astype(F32)
    for index in range(1, z.layer):
        total = total + dbuf[index].astype(F32)
    total = total.astype(BF16).astype(F32)
    for r in range(rd):
        parts = [total[r * 8 : r * 8 + 8, b * 128 : b * 128 + 128] for b in range(3)]
        if r > 0:
            above = total[r * 8 - 8 : r * 8, 256:384]
            parts[0] = parts[0] + jnp.where(masks[0], pltpu.roll(above, 86, 1), 0.0)
        if r < rd - 1:
            below = total[r * 8 + 8 : r * 8 + 16, 0:128]
            parts[2] = parts[2] + jnp.where(masks[2], pltpu.roll(below, 42, 1), 0.0)
        sb2[r] = jnp.concatenate(parts, axis=1)
    for offset in range(1, rd):
        index, where = column(offset)
        s_b1.start(sb2.at[index], b1.at[me], where)
    b1[me] = sb2[me]
    s_b1.arrive()

    image_rows = slab * 8
    grads = jnp.concatenate([b1[slot_ref[0, j]] for j in range(slab)], axis=0)
    lane_s = lax.broadcasted_iota(jnp.int32, (image_rows, 128), 1)
    chunk_s = lax.rem(lax.broadcasted_iota(jnp.int32, (image_rows, 128), 0), 8)
    column_s = lax.rem(lane_s, CHUNK)
    from_left = (column_s == CHUNK - 1) & (chunk_s > 0)
    from_right = (column_s == 0) & (chunk_s < CHUNKS - 1)
    lines = []
    for y in range(ROWS):
        main = jnp.zeros((image_rows, 128), F32)
        for ky in range(3):
            block, j = divmod(y + 2 - ky, 3)
            shift = 42 * (ky - j) % 128
            moved = grads[:, block * 128 : block * 128 + 128]
            moved = moved if shift == 0 else pltpu.roll(moved, shift, 1)
            main = main + jnp.where((lane_s >= 42 * ky) & (lane_s < 42 * ky + 42), moved, 0.0)
        rim = jnp.where(from_left, pltpu.roll(main, 1, 0), 0.0)
        rim = jnp.where(from_right, pltpu.roll(main, image_rows - 1, 0), rim)
        lines.append(jnp.concatenate([main, rim], axis=1).astype(BF16))
    lines.append(jnp.zeros((image_rows, 256), BF16))
    lhs = jnp.concatenate(lines, axis=0)
    spread = mm(lhs, bandb[...])
    for block in range(CHUNK_BLOCKS):
        dact[block] = spread[:, block * 128 : block * 128 + 128]

    def gate(c, carry):
        at = pl.ds(pl.multiple_of(c * wide, 128), wide)
        parts = [
            dact[block, pl.ds(c, z.slab8, stride=8), :] for block in range(CHUNK_BLOCKS)
        ]
        gated = jnp.concatenate(parts, axis=1) * slope[:, at]
        slope[:, at] = gated
        return carry[0] + lanes_sum(gated), carry[1] + lanes_sum(gated * xs[:, at])

    first, second = lax.fori_loop(0, CHUNKS, gate, (zero, zero))
    bs_own[...] = total_rows(first, second)
    for offset in range(1, rd):
        index, where = column(offset)
        s_bst.start(bs_own, bs_buf.at[me], where)
    bs_buf[me] = bs_own[...]
    s_bst.arrive()
    both = group_means(bs_buf)
    one_t = jnp.concatenate([both[:slab]] * 8, axis=0)
    two_t = jnp.concatenate([both[slab:]] * 8, axis=0)

    def finish(c, carry):
        at = pl.ds(pl.multiple_of(c * wide, 128), wide)
        one = jnp.concatenate([one_t] * CHUNK_BLOCKS, axis=1)
        two = jnp.concatenate([two_t] * CHUNK_BLOCKS, axis=1)
        inv = jnp.concatenate([inverse_t] * CHUNK_BLOCKS, axis=1)
        value = inv * (slope[:, at] - one - xs[:, at] * two)
        for y in range(ROWS):
            grad_ref[y, :, at] = value[y * slab : y * slab + slab].astype(BF16)
        return carry

    lax.fori_loop(0, CHUNKS, finish, 0)
    for sender in sems:
        sender.finish()


def body(features, gn_gain, conv_w, patch_w, pos_emb, ln1_gain, qkv_w, out_w, final_gain, head_w, owner_slot):
    slab = features.shape[0]
    rd = lax.axis_size("rows")
    tp = lax.axis_size("tp")
    half_width = qkv_w.shape[2]
    heads_half = half_width // HEAD_DIM
    split_axes = ("grp", "img")
    if heads_half % (lax.axis_size("grp") * lax.axis_size("img")):
        split_axes = ("img",)
    split_sizes = tuple(lax.axis_size(axis) for axis in split_axes)
    planes = math.prod(split_sizes)
    heads = heads_half // planes
    z = Sizes(slab, rd, planes, tp, pos_emb.shape[1], heads * HEAD_DIM, heads, half_width)
    flat = features.shape[3]
    vmem = pl.BlockSpec(memory_space=pltpu.VMEM)
    anys = pl.BlockSpec(memory_space=pl.ANY)
    smem = pl.BlockSpec(memory_space=pltpu.SMEM)
    args = [
        (jnp.transpose(features.reshape(slab, ROWS, flat), (1, 0, 2)), anys),
        (gn_gain.reshape(1, -1), anys),
        (conv_w, anys),
        (patch_w, anys),
        (pos_emb, anys),
        (ln1_gain.reshape(-1, 128), anys),
        (jnp.transpose(qkv_w, (1, 0, 2)), anys),
        (out_w, anys),
        (final_gain.reshape(-1, 128), anys),
        (head_w.reshape(-1, 128), anys),
        (owner_slot, smem),
    ]
    spaces = [anys] * 9
    args += list(zip(tables(z), spaces))
    k, own, width, lay, tok = z.k, z.own, z.width, z.layer, z.tokens
    rows_all, unit = planes * tok, heads * tok
    half_rows = rd * CHUNKS
    two = 2 * slab

    def v(shape, dtype=F32):
        return pltpu.VMEM(shape, dtype)

    scratch = [
        v((ROWS, slab, flat), BF16), v(patch_w.shape, BF16), v((3, own, 256), BF16), v((own, 256), BF16),
        v((3 * PATCH * PATCH, k), BF16), v((32, 18 * 128), BF16), v((256, 7 * 64), BF16), v((384, 2 * k), BF16),
        v((z.pack, 3 * heads * 128), BF16),
        v((1, 64)), v(conv_w.shape, BF16), v(pos_emb.shape, BF16), v((width // 128, 128)), v((width // 128, 128)), v((width // 128, 128)),
        v((tok, k), BF16), v((tok, k), BF16), v((128, 128)), v((two, 2 * z.slab8)),
        v((z.slab8, flat)), v((z.slab8, flat)), v((z.slab8, flat + 256), BF16), v((32, 128)),
        v((1152, 128), BF16), v((256, 896), BF16), v((CHUNKS * z.slab8, 128)),
        v((slab, 8, 384)), v((slab, 8, 384)), v((rd, 8, 384)), v((lay, half_rows, 384), BF16), v((half_rows, 384), BF16),
        v((two, 128)), v((rd, two, 128)), v((8, 128)), v((rd, 8, 128)),
        v((k, z.pack), BF16), v((2, rd) + z.chunk, BF16), v((k, z.pack), BF16), v((k, 3 * heads * 128), BF16),
        v((width, k), BF16), v((width, heads * 128), BF16), v((z.win, k + 128)), v((k, k)),
        v((z.f_rows, 128), BF16), v((z.share, rd, z.f_part, 128), BF16), v((z.o_rows, 128), BF16), v((rd, z.o_rows, 128), BF16),
        v((1, width)),
        v((rows_all, k), BF16), v((rows_all, k)), v((rows_all, 3 * heads * 128), BF16), v((planes, unit, unit)),
        v((z.prow, heads * 128)), v((z.mrows, 128), BF16), v((lay, z.mrows, 128), BF16), v((rows_all, 3 * heads * 128), BF16),
        v((planes, half_rows, 384), BF16), v((lay, half_rows, 384), BF16), v((rd, 8, 384)), v((rd, 8, 384)),
        v((7, z.slab8 * 8, 128)), v((two, 128)), v((rd, two, 128)),
        v((rows_all, 128)), v((z.prow, heads * 128)), v((z.prow, k)),
        pltpu.SemaphoreType.DMA((19,)),
    ]
    for copies in [rd - 1] * 5 + [2 * rd - 2, rd - 1] + [lay - 1] * 3 + [rd - 1] * 2 + [max(planes - 1, 1)] + [rd - 1] * 2 + [max(tp - 1, 1)]:
        scratch += [pltpu.SemaphoreType.DMA((copies,))] * 2
    grad, reward = pl.pallas_call(
        functools.partial(kernel, z, split_axes, split_sizes),
        out_shape=[
            jax.ShapeDtypeStruct((ROWS, slab, flat), BF16),
            jax.ShapeDtypeStruct((1, 1), F32),
        ],
        in_specs=[spec for _, spec in args],
        out_specs=[vmem, vmem],
        scratch_shapes=scratch,
        compiler_params=pltpu.CompilerParams(
            collective_id=0, has_side_effects=True, vmem_limit_bytes=58 * 2**20
        ),
    )(*[value for value, _ in args])
    return jnp.transpose(grad, (1, 0, 2)).reshape(slab, ROWS, 1, flat), reward.reshape(1)


def solution(mesh):
    placed = (
        P(("grp", "img"), "rows", "tp", None),
        P("tp"),
        P(None, None, None, "tp"),
        P("rows", None),
        P(),
        P(),
        P("rows", None, "tp"),
        P("rows", "tp"),
        P(),
        P(),
        P(("grp", "img"), None),
    )
    return jax.shard_map(
        body,
        mesh=mesh,
        in_specs=placed,
        out_specs=(P(("grp", "img"), "rows", "tp", None), P(("grp", "img", "rows"))),
        check_vma=False,
    )
```
